512 devices in a mesh: sec: 4 (over x_lo, core), fsdp: 128 (over y, z, x_hi).
Axes of the slice: x: 4 (x_hi: 2, x_lo: 2; x = x_hi * 2 + x_lo), y: 4, z: 16, core: 2. Of those that a mesh axis runs over, the one named last changes fastest.
Arguments:
- tokens: bfloat16 [65536, 6144], P('fsdp', 'sec'), may hold values from -6 to 6
- grad_out: bfloat16 [65536, 6144], P('fsdp', 'sec'), may hold values from -24 to 24
- gain: float32 [6144], P('sec'), may hold values from 0.1 to 7
- qkv_weight: bfloat16 [6144, 384], P(('sec', 'fsdp')), may hold values from -0.078125 to 0.078125
- out_weight: bfloat16 [128, 6144], P(None, ('sec', 'fsdp')), may hold values from -0.5 to 0.5
Outputs:
- grad_tokens: bfloat16 [65536, 6144], P('fsdp', 'sec')
- grad_qkv: float32 [6144, 384], P(('sec', 'fsdp'))
- grad_outw: float32 [128, 6144], P(None, ('sec', 'fsdp'))
- grad_gain: float32 [6144], P(('sec', 'fsdp'))
The draws below stay inside these ranges and needn't reach their ends.
All inputs are finite; a program needn't handle non-finite values.
Results may differ from the reference program's by a relative error of at most 0.012.
The reference program's roundings to bfloat16 on the way (of `hidden`, `proj`, `probs_b`, `attended`, `grad_att`, `grad_score` and `grad_proj`) count: a program that leaves them out, or rounds other values in their place, can miss the bound.
Values may be sent and summed in bfloat16 or wider, within the bound.
No kernel may reach another device: no remote copies, remote signals or barrier semaphores. Data moves between devices by JAX's collectives and lax.ppermute only.
A program may use at most 64 MiB of HBM per device.

```python
import jax
import jax.numpy as jnp
from jax import lax

D = 6144
HD = 128
PATCHES = 256
IMAGES = 256
TOKENS = 65536


def draw_gain(key, part):
    position = jnp.arange(D, dtype=jnp.float32) / (D - 1)
    base = jnp.exp(jnp.log(0.4) + jnp.log(10.0) * position)
    rough = jax.random.uniform(key, (D,), jnp.float32, 0.7, 1.3)
    return (base * rough).astype(jnp.float32)


def strengthened(drawn, stream_key, source, target, shards_of, factor):
    def block_of(axis_at):
        return (jnp.arange(drawn.shape[axis_at]) // (drawn.shape[axis_at] // shards_of)).reshape((-1,) + (1,) * (drawn.ndim - 1 - axis_at))

    one_side = jax.random.permutation(stream_key, shards_of)[block_of(target)]
    far = (block_of(target) + shards_of // 2) % shards_of
    return jnp.where((block_of(source) == one_side) | (block_of(source) == far), factor * drawn, drawn)


def shard_levels(key, dims, split, smallest, largest):
    level = 1.0
    for dim, shards_of in split:
        steps = jax.random.uniform(jax.random.fold_in(jax.random.fold_in(key, 6), dim), (shards_of,), jnp.float32, smallest / len(split), largest / len(split))
        level = level * jnp.repeat(jnp.exp(steps), dims[dim] // shards_of).reshape((-1,) + (1,) * (len(dims) - 1 - dim))
    return level


def noise(own_key, extent, deviation, bound, split=(), kind=jnp.bfloat16):
    result = deviation * jax.random.normal(own_key, extent, jnp.float32)
    if split:
        result = result * shard_levels(own_key, extent, split, -0.22, 0.18)
    return jnp.clip(result, -bound, bound).astype(kind)


def noise_with(stream_key, dims, width, most, pieces, heavy, kind=jnp.bfloat16):
    entries = width * jax.random.normal(stream_key, dims, jnp.float32)
    if pieces:
        entries = entries * shard_levels(stream_key, dims, pieces, -0.22, 0.18)
    return jnp.clip(strengthened(entries, jax.random.fold_in(stream_key, 3), *heavy), -most, most).astype(kind)


def setup_inputs(seed: int = 0) -> dict:
    keys = jax.random.split(jax.random.key(seed), 6)
    return {
        "tokens": noise(keys[0], (TOKENS, D), 1.0, 6.0, ((0, 128), (1, 4))),
        "grad_out": noise_with(keys[1], (TOKENS, D), 1.0, 24.0, ((0, 128), (1, 4)), (0, 1, 128, 5.5)),
        "gain": draw_gain(jax.random.fold_in(keys[5], 71), 0),
        "qkv_weight": noise(keys[3], (D, 3 * HD), D ** -0.5, 0.078125, ((0, 512),)),
        "out_weight": noise(keys[4], (HD, D), HD ** -0.5, 0.5, ((1, 512),)),
    }


EPS = 1e-06

def reference(tokens, grad_out, gain, qkv_weight, out_weight):
    tok_float = tokens.astype(jnp.float32)
    row_mean = lax.optimization_barrier(jnp.sum(tok_float, axis=1)) / D
    row_var = lax.optimization_barrier(jnp.sum(tok_float * tok_float, axis=1)) / D - row_mean * row_mean
    inv_std = lax.rsqrt(row_var + EPS)
    normed = (tok_float - row_mean[:, None]) * inv_std[:, None]
    hidden = (normed * gain[None, :]).astype(jnp.bfloat16)
    proj = jnp.dot(hidden, qkv_weight, preferred_element_type=jnp.float32).astype(jnp.bfloat16)
    parts = proj.reshape(IMAGES, PATCHES, 3, HD).astype(jnp.float32)
    query, key_in, value = (parts[:, :, 0], parts[:, :, 1], parts[:, :, 2])
    scale = 1.0 / HD ** 0.5
    scores = jnp.einsum('ipd,iqd->ipq', query, key_in) * scale
    probs = jax.nn.softmax(scores, axis=-1)
    probs_b = probs.astype(jnp.bfloat16)
    attended = jnp.einsum('ipq,iqd->ipd', probs_b.astype(jnp.float32), value).astype(jnp.bfloat16)
    attended = attended.reshape(TOKENS, HD)
    grad_outw = jnp.dot(attended.T, grad_out, preferred_element_type=jnp.float32)
    grad_att = jnp.dot(grad_out, out_weight.T, preferred_element_type=jnp.float32).astype(jnp.bfloat16)
    grad_att3 = grad_att.reshape(IMAGES, PATCHES, HD).astype(jnp.float32)
    grad_prob = jnp.einsum('ipd,iqd->ipq', grad_att3, value)
    grad_score = (probs * (grad_prob - lax.optimization_barrier(jnp.sum(grad_prob * probs, axis=-1, keepdims=True))) * scale).astype(jnp.bfloat16)
    score_f = grad_score.astype(jnp.float32)
    grad_query = jnp.einsum('ipq,iqd->ipd', score_f, key_in)
    grad_key = jnp.einsum('ipq,ipd->iqd', score_f, query)
    grad_value = jnp.einsum('ipq,ipd->iqd', probs_b.astype(jnp.float32), grad_att3)
    grad_proj = jnp.stack([grad_query, grad_key, grad_value], axis=2).reshape(TOKENS, 3 * HD).astype(jnp.bfloat16)
    grad_qkv = jnp.dot(hidden.T, grad_proj, preferred_element_type=jnp.float32)
    grad_hidden = jnp.dot(grad_proj, qkv_weight.T, preferred_element_type=jnp.float32)
    grad_gain = lax.optimization_barrier(jnp.sum(grad_hidden * normed, axis=0))
    grad_normed = grad_hidden * gain[None, :]
    first = lax.optimization_barrier(jnp.sum(grad_normed, axis=1)) / D
    second = lax.optimization_barrier(jnp.sum(grad_normed * normed, axis=1)) / D
    grad_tokens = grad_out.astype(jnp.float32) + inv_std[:, None] * (grad_normed - first[:, None] - normed * second[:, None])
    return (grad_tokens.astype(jnp.bfloat16), grad_qkv, grad_outw, grad_gain)
```

```python
import jax
import jax.numpy as jnp
from jax import lax
from jax.sharding import Mesh
from jax.sharding import PartitionSpec as P

PATCHES = 256


EPS = 1e-06

SEC = ("xlo", "core")
FSDP = ("y", "z", "xhi")
NEAR = ("y", "xhi")


def gather_weights(block):
    rows, width = block.shape
    ny, nz, nx = (lax.axis_size(a) for a in FSDP)
    padded = jnp.pad(block, ((0, -rows % 16), (0, 0)))
    along_z = lax.all_to_all(
        jnp.broadcast_to(padded[None], (nz,) + padded.shape), "z", 0, 0
    )[:, :rows].reshape(nz * rows, width)
    near = lax.all_to_all(
        jnp.broadcast_to(along_z[None], (ny * nx,) + along_z.shape), NEAR, 0, 0
    )
    near = near.reshape(ny, nx, nz, rows, width).transpose(0, 2, 1, 3, 4)
    return near.reshape(ny * nz * nx * rows, width)


def scatter_sums(partial):
    ny, nz, nx = (lax.axis_size(a) for a in FSDP)
    total, width = partial.shape
    rows = total // (ny * nz * nx)
    near = partial.reshape(ny, nz, nx, rows, width).transpose(0, 2, 1, 3, 4)
    near = near.reshape(ny * nx, nz * rows, width).astype(jnp.bfloat16)
    near = lax.all_to_all(near, NEAR, 0, 0)
    summed = jnp.sum(near.astype(jnp.float32), axis=0).reshape(nz, rows, width)
    summed = jnp.pad(summed, ((0, 0), (0, -rows % 16), (0, 0))).astype(jnp.bfloat16)
    along_z = lax.all_to_all(summed, "z", 0, 0)[:, :rows]
    return jnp.sum(along_z.astype(jnp.float32), axis=0)


def sum_over_sec(partial):
    rows, width = partial.shape
    half = lax.all_to_all(partial.reshape(2, rows // 2, width), "core", 0, 0)
    half = half[0] + half[1]
    quarter = lax.all_to_all(half.reshape(2, rows // 4, width), "xlo", 0, 0)
    quarter = (quarter[0] + quarter[1]).astype(jnp.bfloat16)
    half = lax.all_gather(quarter, "xlo", axis=0, tiled=True)
    return lax.all_gather(half, "core", axis=0, tiled=True)


def on_device(tokens, grad_out, gain, qkv_weight, out_weight):
    tok_rows, local_width = tokens.shape
    model_width = local_width * lax.axis_size(SEC)
    head_size = out_weight.shape[0]
    images = tok_rows // PATCHES
    own_rows = qkv_weight.shape[0]

    weights = gather_weights(jnp.concatenate([qkv_weight, out_weight.T], axis=1))
    qkv_all = weights[:, : 3 * head_size]
    outw_all = weights[:, 3 * head_size :]

    tok_float = tokens.astype(jnp.float32)
    gain_high = gain.astype(jnp.bfloat16)
    gain_low = (gain - gain_high.astype(jnp.float32)).astype(jnp.bfloat16)
    weight_sums = jnp.dot(
        jnp.stack([gain_high, gain_low]), qkv_all, preferred_element_type=jnp.float32
    ).sum(axis=0)
    row_sums, row_squares, weight_sums = lax.psum(
        (jnp.sum(tok_float, axis=1), jnp.sum(tok_float * tok_float, axis=1), weight_sums), SEC
    )
    row_mean = row_sums / model_width
    row_var = row_squares / model_width - row_mean * row_mean
    inv_std = lax.rsqrt(row_var + EPS)
    normed = (tok_float - row_mean[:, None]) * inv_std[:, None]
    hidden = (normed * gain[None, :]).astype(jnp.bfloat16)
    proj_partial = jnp.dot(hidden, qkv_all, preferred_element_type=jnp.float32)
    att_partial = jnp.dot(grad_out, outw_all, preferred_element_type=jnp.float32)
    both = sum_over_sec(jnp.concatenate([proj_partial, att_partial], axis=1))
    proj = both[:, : 3 * head_size]
    grad_att3 = both[:, 3 * head_size :].reshape(images, PATCHES, head_size)
    parts = proj.reshape(images, PATCHES, 3, head_size)
    query, key_in, value = (parts[:, :, 0], parts[:, :, 1], parts[:, :, 2])
    scale = 1.0 / head_size**0.5
    scores = jnp.einsum("ipd,iqd->ipq", query, key_in, preferred_element_type=jnp.float32) * scale
    probs = jax.nn.softmax(scores, axis=-1)
    probs_b = probs.astype(jnp.bfloat16)
    attended = jnp.einsum(
        "ipq,iqd->ipd", probs_b, value, preferred_element_type=jnp.float32
    ).astype(jnp.bfloat16)
    attended = attended.reshape(tok_rows, head_size)
    grad_prob = jnp.einsum("ipd,iqd->ipq", grad_att3, value, preferred_element_type=jnp.float32)
    grad_score = (
        probs * (grad_prob - jnp.sum(grad_prob * probs, axis=-1, keepdims=True)) * scale
    ).astype(jnp.bfloat16)
    grad_query = jnp.einsum("ipq,iqd->ipd", grad_score, key_in, preferred_element_type=jnp.float32)
    grad_key = jnp.einsum("ipq,ipd->iqd", grad_score, query, preferred_element_type=jnp.float32)
    grad_value = jnp.einsum("ipq,ipd->iqd", probs_b, grad_att3, preferred_element_type=jnp.float32)
    grad_proj = (
        jnp.stack([grad_query, grad_key, grad_value], axis=2)
        .reshape(tok_rows, 3 * head_size)
        .astype(jnp.bfloat16)
    )
    over_rows = (((0,), (0,)), ((), ()))
    local_qkv = lax.dot_general(hidden, grad_proj, over_rows, preferred_element_type=jnp.float32)
    local_outw = lax.dot_general(grad_out, attended, over_rows, preferred_element_type=jnp.float32)
    summed = scatter_sums(jnp.concatenate([local_qkv, local_outw], axis=1))
    grad_qkv = summed[:, : 3 * head_size]
    grad_outw = summed[:, 3 * head_size :].T
    own = lax.axis_index(FSDP) * own_rows
    grad_gain = jnp.sum(qkv_weight.astype(jnp.float32) * grad_qkv, axis=1) / lax.dynamic_slice(
        gain, (own,), (own_rows,)
    )

    grad_hidden = lax.dot_general(
        grad_proj, qkv_all, (((1,), (1,)), ((), ())), preferred_element_type=jnp.float32
    )
    proj_grad = grad_proj.astype(jnp.float32)
    first = jnp.sum(proj_grad * weight_sums[None, :], axis=1) / model_width
    second = jnp.sum(proj_grad * proj.astype(jnp.float32), axis=1) / model_width
    grad_normed = grad_hidden * gain[None, :]
    grad_tokens = grad_out.astype(jnp.float32) + inv_std[:, None] * (
        grad_normed - first[:, None] - normed * second[:, None]
    )
    return (grad_tokens.astype(jnp.bfloat16), grad_qkv, grad_outw, grad_gain)


def solution(mesh):
    fine = Mesh(mesh.devices.reshape(2, 2, 4, 16, 2), SEC + FSDP)
    placed = (
        P(FSDP, SEC),
        P(FSDP, SEC),
        P(SEC),
        P(SEC + FSDP, None),
        P(None, SEC + FSDP),
    )
    return jax.shard_map(
        on_device,
        mesh=fine,
        in_specs=placed,
        out_specs=(
            P(FSDP, SEC),
            P(SEC + FSDP, None),
            P(None, SEC + FSDP),
            P(SEC + FSDP),
        ),
        check_vma=False,
    )
```

```python
import functools

import jax
import jax.numpy as jnp
from jax import lax
from jax.experimental import pallas as pl
from jax.experimental.pallas import tpu as pltpu
from jax.sharding import Mesh
from jax.sharding import PartitionSpec as P

PATCHES = 256


EPS = 1e-06

SEC = ("xlo", "core")
FSDP = ("y", "z", "xhi")
NEAR = ("y", "xhi")
LANES = 128
VMEM_LIMIT = 28 * 1024 * 1024

nt_dims = (((1,), (1,)), ((), ()))
tn_dims = (((0,), (0,)), ((), ()))


def dot(a, b, dims=(((1,), (0,)), ((), ()))):
    return lax.dot_general(a, b, dims, preferred_element_type=jnp.float32)


def by_rows(index, rows):
    return lax.shift_right_logical(index * (65536 // rows + 1), jnp.full_like(index, 16))


def picks(shape, source_of_row):
    row = lax.broadcasted_iota(jnp.int32, shape, 0)
    column = lax.broadcasted_iota(jnp.int32, shape, 1)
    return (column == source_of_row(row)).astype(jnp.float32).astype(jnp.bfloat16)


def unpack_block(rows, blocks, column_block):
    return lambda i: i + by_rows(i, rows) * (rows * (blocks - 1)) + column_block * rows


def near_order(rows, nz):
    def source(i):
        z = by_rows(i, 2 * rows)
        rest = i - z * 2 * rows
        high = (rest >= rows).astype(jnp.int32)
        return high * (nz * rows) + z * rows + rest - high * rows

    return source


def spread_kernel(rows, x_ref, o_ref):
    copies, span, width = o_ref.shape
    blocks = width // LANES
    x = x_ref[...]
    for b in range(blocks):
        pick = picks((span, x.shape[0]), unpack_block(rows, blocks, b))
        part = dot(pick, x).astype(jnp.bfloat16)
        for k in range(copies):
            o_ref[k, :, b * LANES : (b + 1) * LANES] = part


def project_kernel(
    rows, nz, near_ref, hidden_ref, gout_ref, gain_ref, w_ref, partial_ref, sums_ref
):
    ny = near_ref.shape[0]
    span = near_ref.shape[1] * near_ref.shape[2]
    heads = hidden_ref.shape[1] // ny
    width = near_ref.shape[3]
    cut = width - LANES
    pick = picks((span, span), near_order(rows, nz))
    sums = jnp.zeros(sums_ref.shape, jnp.float32)
    for y in range(ny):
        block = near_ref[y].reshape(span, width)
        natural = dot(pick, block).astype(jnp.bfloat16)
        w_ref[y * span : (y + 1) * span, :] = natural
        sums = sums + dot(gain_ref[:, y * span : (y + 1) * span], natural[:, :cut])
    sums_ref[...] = sums
    partial_ref[:, :cut] = dot(hidden_ref[...], w_ref[:, :cut])
    partial_ref[:, cut:] = dot(gout_ref[...], w_ref[:, cut:])


def attend_kernel(rows, nz, both_ref, hidden_ref, gout_ref, near_ref, gproj_ref, att_ref):
    ny = near_ref.shape[0]
    width = near_ref.shape[3]
    span = near_ref.shape[1] * near_ref.shape[2]
    head = LANES
    scale = 1.0 / head**0.5
    for image in range(both_ref.shape[0] // PATCHES):
        at = slice(image * PATCHES, (image + 1) * PATCHES)
        query = both_ref[at, :head]
        key_in = both_ref[at, head : 2 * head]
        value = both_ref[at, 2 * head : 3 * head]
        grad_att = both_ref[at, 3 * head :]
        scores = dot(query, key_in, nt_dims) * scale
        raised = jnp.exp(scores - jnp.max(scores, axis=1, keepdims=True))
        probs = raised / jnp.sum(raised, axis=1, keepdims=True)
        probs_b = probs.astype(jnp.bfloat16)
        att_ref[at, :] = dot(probs_b, value).astype(jnp.bfloat16)
        grad_prob = dot(grad_att, value, nt_dims)
        inner = jnp.sum(grad_prob * probs, axis=1, keepdims=True)
        grad_score = (probs * (grad_prob - inner) * scale).astype(jnp.bfloat16)
        gproj_ref[at, :head] = dot(grad_score, key_in).astype(jnp.bfloat16)
        gproj_ref[at, head : 2 * head] = dot(grad_score, query, tn_dims).astype(jnp.bfloat16)
        gproj_ref[at, 2 * head :] = dot(probs_b, grad_att, tn_dims).astype(jnp.bfloat16)
    row = lax.broadcasted_iota(jnp.int32, (span, span), 0)
    column = lax.broadcasted_iota(jnp.int32, (span, span), 1)
    pick = (row == near_order(rows, nz)(column)).astype(jnp.float32).astype(jnp.bfloat16)
    cut = width - head
    for y in range(ny):
        at = slice(y * span, (y + 1) * span)
        qkv_t = dot(gproj_ref[...], hidden_ref[:, at], tn_dims).astype(jnp.bfloat16)
        out_t = dot(att_ref[...], gout_ref[:, at], tn_dims).astype(jnp.bfloat16)
        sent = dot(pick, qkv_t, nt_dims).astype(jnp.bfloat16)
        near_ref[y, :, :, :cut] = sent.reshape(2, span // 2, cut)
        sent = dot(pick, out_t, nt_dims).astype(jnp.bfloat16)
        near_ref[y, :, :, cut:] = sent.reshape(2, span // 2, head)


def fold_kernel(rows, near_ref, o_ref):
    copies, span, width = near_ref.shape
    blocks = width // LANES
    total = near_ref[0].astype(jnp.float32)
    for k in range(1, copies):
        total = total + near_ref[k].astype(jnp.float32)
    total = total.astype(jnp.bfloat16)
    row = lax.broadcasted_iota(jnp.int32, (o_ref.shape[0], span), 0)
    column = lax.broadcasted_iota(jnp.int32, (o_ref.shape[0], span), 1)
    packed = jnp.zeros(o_ref.shape, jnp.float32)
    for b in range(blocks):
        pick = row == unpack_block(rows, blocks, b)(column)
        pick = pick.astype(jnp.float32).astype(jnp.bfloat16)
        packed = packed + dot(pick, total[:, b * LANES : (b + 1) * LANES])
    o_ref[...] = packed.astype(jnp.bfloat16)


def call(kernel, out_shape, flops, moved, **more):
    return pl.pallas_call(
        kernel,
        out_shape=out_shape,
        compiler_params=pltpu.CompilerParams(vmem_limit_bytes=VMEM_LIMIT),
        cost_estimate=pl.CostEstimate(flops=flops, bytes_accessed=moved, transcendentals=0),
        **more,
    )


def array(shape, dtype=jnp.bfloat16):
    return jax.ShapeDtypeStruct(shape, dtype)


def on_device(tokens, grad_out, gain, qkv_weight, out_weight):
    tok_rows, local_width = tokens.shape
    model_width = local_width * lax.axis_size(SEC)
    head = out_weight.shape[0]
    rows = qkv_weight.shape[0]
    ny, nz, nx = (lax.axis_size(a) for a in FSDP)
    cut = 3 * head
    width = cut + head
    blocks = width // LANES

    packed = jnp.concatenate(
        [qkv_weight.reshape(rows, 3, head).transpose(1, 0, 2), out_weight.T[None]], axis=0
    ).reshape(blocks * rows, LANES)
    along_z = lax.all_to_all(
        jnp.broadcast_to(packed[None], (nz,) + packed.shape), "z", 0, 0
    ).reshape(nz * blocks * rows, LANES)

    tok_float = tokens.astype(jnp.float32)
    row_sums, row_squares = lax.psum(
        (jnp.sum(tok_float, axis=1), jnp.sum(tok_float * tok_float, axis=1)), SEC
    )

    spread = call(
        functools.partial(spread_kernel, rows),
        array((ny * nx, nz * rows, width)),
        300_000_000,
        2_000_000,
    )(along_z)
    near = lax.all_to_all(spread, NEAR, 0, 0)

    row_mean = row_sums / model_width
    row_var = row_squares / model_width - row_mean * row_mean
    inv_std = lax.rsqrt(row_var + EPS)
    normed = (tok_float - row_mean[:, None]) * inv_std[:, None]
    hidden = (normed * gain[None, :]).astype(jnp.bfloat16)

    gain_high = gain.astype(jnp.bfloat16)
    gain_low = (gain - gain_high.astype(jnp.float32)).astype(jnp.bfloat16)
    gains = jnp.concatenate(
        [gain_high[None], gain_low[None], jnp.zeros((14, local_width), jnp.bfloat16)], axis=0
    )
    weights, partial, weight_sums = call(
        functools.partial(project_kernel, rows, nz),
        (
            array((local_width, width)),
            array((tok_rows, width), jnp.float32),
            array((16, cut), jnp.float32),
        ),
        1_500_000_000,
        8_000_000,
    )(near.reshape(ny, nx, nz * rows, width), hidden, grad_out, gains)

    half = lax.all_to_all(partial.reshape(2, tok_rows // 2, width), "core", 0, 0)
    half = half[0] + half[1]
    half = (half + lax.ppermute(half, "xlo", [(0, 1), (1, 0)])).astype(jnp.bfloat16)
    both = lax.all_gather(half, "core", axis=0, tiled=True)

    sent, grad_proj = call(
        functools.partial(attend_kernel, rows, nz),
        (array((ny, nx, nz * rows, width)), array((tok_rows, cut))),
        1_800_000_000,
        6_000_000,
        scratch_shapes=[pltpu.VMEM((tok_rows, head), jnp.bfloat16)],
    )(both, hidden, grad_out)

    received = lax.all_to_all(sent.reshape(ny * nx, nz * rows, width), NEAR, 0, 0)
    folded = call(
        functools.partial(fold_kernel, rows),
        array((nz * blocks * rows, LANES)),
        300_000_000,
        2_000_000,
    )(received)
    folded = lax.all_to_all(folded.reshape(nz, blocks * rows, LANES), "z", 0, 0)
    summed = jnp.sum(folded.astype(jnp.float32), axis=0).reshape(blocks, rows, LANES)
    grad_qkv = summed[:3].transpose(1, 0, 2).reshape(rows, cut)
    grad_outw = summed[3].T
    own = lax.axis_index(FSDP) * rows
    grad_gain = jnp.sum(qkv_weight.astype(jnp.float32) * grad_qkv, axis=1) / lax.dynamic_slice(
        gain, (own,), (rows,)
    )

    weight_sums = lax.psum(weight_sums[0] + weight_sums[1], SEC)
    grad_hidden = lax.dot_general(
        grad_proj, weights[:, :cut], nt_dims, preferred_element_type=jnp.float32
    )
    proj_grad = grad_proj.astype(jnp.float32)
    first = jnp.sum(proj_grad * weight_sums[None, :], axis=1) / model_width
    second = jnp.sum(proj_grad * both[:, :cut].astype(jnp.float32), axis=1) / model_width
    grad_normed = grad_hidden * gain[None, :]
    grad_tokens = grad_out.astype(jnp.float32) + inv_std[:, None] * (
        grad_normed - first[:, None] - normed * second[:, None]
    )
    return (grad_tokens.astype(jnp.bfloat16), grad_qkv, grad_outw, grad_gain)


def solution(mesh):
    fine = Mesh(mesh.devices.reshape(2, 2, 4, 16, 2), SEC + FSDP)
    placed = (
        P(FSDP, SEC),
        P(FSDP, SEC),
        P(SEC),
        P(SEC + FSDP, None),
        P(None, SEC + FSDP),
    )
    return jax.shard_map(
        on_device,
        mesh=fine,
        in_specs=placed,
        out_specs=(
            P(FSDP, SEC),
            P(SEC + FSDP, None),
            P(None, SEC + FSDP),
            P(SEC + FSDP),
        ),
        check_vma=False,
    )
```

```python
import functools

import jax
import jax.numpy as jnp
from jax import lax
from jax.experimental import pallas as pl
from jax.experimental.pallas import tpu as pltpu
from jax.sharding import Mesh
from jax.sharding import PartitionSpec as P

PATCHES = 256


EPS = 1e-06

SEC = ("xlo", "core")
FSDP = ("y", "z", "xhi")
NEAR = ("y", "xhi")
LANES = 128
VMEM_LIMIT = 28 * 1024 * 1024

nt_dims = (((1,), (1,)), ((), ()))
tn_dims = (((0,), (0,)), ((), ()))


def dot(a, b, dims=(((1,), (0,)), ((), ()))):
    return lax.dot_general(a, b, dims, preferred_element_type=jnp.float32)


def by_rows(index, rows):
    return lax.shift_right_logical(index * (65536 // rows + 1), jnp.full_like(index, 16))


def picks(shape, source_of_row):
    row = lax.broadcasted_iota(jnp.int32, shape, 0)
    column = lax.broadcasted_iota(jnp.int32, shape, 1)
    return (column == source_of_row(row)).astype(jnp.float32).astype(jnp.bfloat16)


def unpack_block(rows, blocks, column_block):
    return lambda i: i + by_rows(i, rows) * (rows * (blocks - 1)) + column_block * rows


def near_order(rows, nz):
    def source(i):
        z = by_rows(i, 2 * rows)
        rest = i - z * 2 * rows
        high = (rest >= rows).astype(jnp.int32)
        return high * (nz * rows) + z * rows + rest - high * rows

    return source


def pack_kernel(qkv_ref, out_t_ref, o_ref):
    copies, span, _ = o_ref.shape
    rows = qkv_ref.shape[0]
    blocks = span // rows
    packed = jnp.zeros((span, LANES), jnp.float32)
    for b in range(blocks):
        pick = picks((span, rows), lambda i: i - b * rows)
        last = b == blocks - 1
        block = out_t_ref[...] if last else qkv_ref[:, b * LANES : (b + 1) * LANES]
        packed = packed + dot(pick, block)
    packed = packed.astype(jnp.bfloat16)
    for k in range(copies):
        o_ref[k] = packed


def spread_kernel(rows, model_width, x_ref, stats_ref, o_ref, norm_ref):
    mean = stats_ref[0:1] / model_width
    norm_ref[0:1] = mean
    norm_ref[1:2] = lax.rsqrt(stats_ref[1:2] / model_width - mean * mean + EPS)
    copies, span, width = o_ref.shape
    blocks = width // LANES
    x = x_ref[...]
    for b in range(blocks):
        pick = picks((span, x.shape[0]), unpack_block(rows, blocks, b))
        part = dot(pick, x).astype(jnp.bfloat16)
        for k in range(copies):
            o_ref[k, :, b * LANES : (b + 1) * LANES] = part


def project_kernel(
    rows, nz, near_ref, hidden_ref, gout_hbm, gain_ref, w_ref, partial_ref, gout_ref, sem
):
    fetch = pltpu.make_async_copy(gout_hbm, gout_ref, sem)
    fetch.start()
    ny = near_ref.shape[0]
    span = near_ref.shape[1] * near_ref.shape[2]
    width = near_ref.shape[3]
    cut = width - LANES
    half = hidden_ref.shape[0] // 2
    pick = picks((span, span), near_order(rows, nz))
    sums = jnp.zeros((gain_ref.shape[0], cut), jnp.float32)
    for y in range(ny):
        block = near_ref[y].reshape(span, width)
        natural = dot(pick, block).astype(jnp.bfloat16)
        w_ref[y * span : (y + 1) * span, :] = natural
        sums = sums + dot(gain_ref[:, y * span : (y + 1) * span], natural[:, :cut])
    for h in range(2):
        at = slice(h * half, (h + 1) * half)
        partial_ref[h, half:, :cut] = sums[:8]
        partial_ref[h, half:, cut:] = jnp.zeros((8, LANES), jnp.float32)
        partial_ref[h, :half, :cut] = dot(hidden_ref[at, :], w_ref[:, :cut])
    fetch.wait()
    for h in range(2):
        at = slice(h * half, (h + 1) * half)
        partial_ref[h, :half, cut:] = dot(gout_ref[at, :], w_ref[:, cut:])


def attend_kernel(
    rows, nz, both_ref, hidden_ref, gout_hbm, near_hbm, gproj_ref, att_ref, gout_ref, near_ref, sem
):
    ny = near_ref.shape[0]
    fetch = pltpu.make_async_copy(gout_hbm, gout_ref, sem.at[ny])
    fetch.start()
    width = near_ref.shape[3]
    span = near_ref.shape[1] * near_ref.shape[2]
    head = LANES
    scale = 1.0 / head**0.5
    for image in range(both_ref.shape[0] // PATCHES):
        at = slice(image * PATCHES, (image + 1) * PATCHES)
        query = both_ref[at, :head]
        key_in = both_ref[at, head : 2 * head]
        value = both_ref[at, 2 * head : 3 * head]
        grad_att = both_ref[at, 3 * head :]
        scores = dot(query, key_in, nt_dims) * scale
        raised = jnp.exp(scores - jnp.max(scores, axis=1, keepdims=True))
        probs = raised / jnp.sum(raised, axis=1, keepdims=True)
        probs_b = probs.astype(jnp.bfloat16)
        att_ref[at, :] = dot(probs_b, value).astype(jnp.bfloat16)
        grad_prob = dot(grad_att, value, nt_dims)
        inner = jnp.sum(grad_prob * probs, axis=1, keepdims=True)
        grad_score = (probs * (grad_prob - inner) * scale).astype(jnp.bfloat16)
        gproj_ref[at, :head] = dot(grad_score, key_in).astype(jnp.bfloat16)
        gproj_ref[at, head : 2 * head] = dot(grad_score, query, tn_dims).astype(jnp.bfloat16)
        gproj_ref[at, 2 * head :] = dot(probs_b, grad_att, tn_dims).astype(jnp.bfloat16)
    row = lax.broadcasted_iota(jnp.int32, (span, span), 0)
    column = lax.broadcasted_iota(jnp.int32, (span, span), 1)
    pick = (row == near_order(rows, nz)(column)).astype(jnp.float32).astype(jnp.bfloat16)
    cut = width - head
    fetch.wait()
    stores = []
    for y in range(ny):
        at = slice(y * span, (y + 1) * span)
        qkv_t = dot(gproj_ref[...], hidden_ref[:, at], tn_dims).astype(jnp.bfloat16)
        out_t = dot(att_ref[...], gout_ref[:, at], tn_dims).astype(jnp.bfloat16)
        sent = dot(pick, qkv_t, nt_dims).astype(jnp.bfloat16)
        near_ref[y, :, :, :cut] = sent.reshape(2, span // 2, cut)
        sent = dot(pick, out_t, nt_dims).astype(jnp.bfloat16)
        near_ref[y, :, :, cut:] = sent.reshape(2, span // 2, head)
        stores.append(pltpu.make_async_copy(near_ref.at[y], near_hbm.at[y], sem.at[y]))
        stores[y].start()
    for store in stores:
        store.wait()


def fold_kernel(rows, near_ref, o_ref):
    copies, span, width = near_ref.shape
    blocks = width // LANES
    total = near_ref[0].astype(jnp.float32)
    for k in range(1, copies):
        total = total + near_ref[k].astype(jnp.float32)
    total = total.astype(jnp.bfloat16)
    row = lax.broadcasted_iota(jnp.int32, (o_ref.shape[0], span), 0)
    column = lax.broadcasted_iota(jnp.int32, (o_ref.shape[0], span), 1)
    packed = jnp.zeros(o_ref.shape, jnp.float32)
    for b in range(blocks):
        pick = row == unpack_block(rows, blocks, b)(column)
        pick = pick.astype(jnp.float32).astype(jnp.bfloat16)
        packed = packed + dot(pick, total[:, b * LANES : (b + 1) * LANES])
    o_ref[...] = packed.astype(jnp.bfloat16)


def finish_kernel(x_ref, qkv_ref, gain_ref, grad_ref, out_t_ref, gg_ref):
    rows = qkv_ref.shape[0]
    copies, span, _ = x_ref.shape
    x = x_ref[...].reshape(copies * span, LANES)
    blocks = span // rows
    row = lax.broadcasted_iota(jnp.int32, (rows, copies * span), 0)
    column = lax.broadcasted_iota(jnp.int32, (rows, copies * span), 1)
    within = column - by_rows(column, span) * span
    products = jnp.zeros((rows, LANES), jnp.float32)
    for b in range(blocks):
        pick = (within == row + b * rows).astype(jnp.float32).astype(jnp.bfloat16)
        part = dot(pick, x)
        if b == blocks - 1:
            out_t_ref[...] = part
        else:
            at = slice(b * LANES, (b + 1) * LANES)
            grad_ref[:, at] = part
            products = products + part * qkv_ref[:, at].astype(jnp.float32)
    gg_ref[...] = jnp.sum(products, axis=1, keepdims=True) / gain_ref[...]


def call(kernel, out_shape, flops, moved, **more):
    return pl.pallas_call(
        kernel,
        out_shape=out_shape,
        compiler_params=pltpu.CompilerParams(vmem_limit_bytes=VMEM_LIMIT),
        cost_estimate=pl.CostEstimate(flops=flops, bytes_accessed=moved, transcendentals=0),
        **more,
    )


def array(shape, dtype=jnp.bfloat16):
    return jax.ShapeDtypeStruct(shape, dtype)


def on_device(tokens, grad_out, gain, qkv_weight, out_weight):
    tok_rows, local_width = tokens.shape
    model_width = local_width * lax.axis_size(SEC)
    head = out_weight.shape[0]
    rows = qkv_weight.shape[0]
    ny, nz, nx = (lax.axis_size(a) for a in FSDP)
    cut = 3 * head
    width = cut + head
    blocks = width // LANES

    packed = call(pack_kernel, array((nz, blocks * rows, LANES)), 1_000_000, 200_000)(
        qkv_weight, out_weight.T
    )
    along_z = lax.all_to_all(packed, "z", 0, 0).reshape(nz * blocks * rows, LANES)

    tok_float = tokens.astype(jnp.float32)
    stats = lax.psum(
        jnp.stack([jnp.sum(tok_float, axis=1), jnp.sum(tok_float * tok_float, axis=1)]), SEC
    )

    spread, norms = call(
        functools.partial(spread_kernel, rows, model_width),
        (array((ny * nx, nz * rows, width)), array((2, tok_rows), jnp.float32)),
        300_000_000,
        2_000_000,
    )(along_z, stats)
    near = lax.all_to_all(spread, NEAR, 0, 0)

    row_mean, inv_std = norms[0], norms[1]
    normed = (tok_float - row_mean[:, None]) * inv_std[:, None]
    hidden = (normed * gain[None, :]).astype(jnp.bfloat16)

    gain_high = gain.astype(jnp.bfloat16)
    gain_low = (gain - gain_high.astype(jnp.float32)).astype(jnp.bfloat16)
    gains = jnp.concatenate(
        [gain_high[None], gain_low[None], jnp.zeros((14, local_width), jnp.bfloat16)], axis=0
    )
    grad_out_hbm = pltpu.with_memory_space_constraint(grad_out, pltpu.HBM)
    in_hbm = pl.BlockSpec(memory_space=pltpu.HBM)
    in_vmem = pl.BlockSpec(memory_space=pltpu.VMEM)
    half_rows = tok_rows // 2
    weights, partial = call(
        functools.partial(project_kernel, rows, nz),
        (array((local_width, width)), array((2, half_rows + 8, width), jnp.float32)),
        1_500_000_000,
        8_000_000,
        in_specs=[in_vmem, in_vmem, in_hbm, in_vmem],
        scratch_shapes=[
            pltpu.VMEM((tok_rows, local_width), jnp.bfloat16),
            pltpu.SemaphoreType.DMA,
        ],
    )(near.reshape(ny, nx, nz * rows, width), hidden, grad_out_hbm, gains)

    half = lax.all_to_all(partial, "core", 0, 0)
    half = half[0] + half[1]
    half = half + lax.ppermute(half, "xlo", [(0, 1), (1, 0)])
    weight_sums = half[half_rows, :cut] + half[half_rows + 1, :cut]
    both = lax.all_gather(half[:half_rows].astype(jnp.bfloat16), "core", axis=0, tiled=True)

    sent, grad_proj = call(
        functools.partial(attend_kernel, rows, nz),
        (pltpu.HBM((ny, nx, nz * rows, width), jnp.bfloat16), array((tok_rows, cut))),
        1_800_000_000,
        6_000_000,
        in_specs=[in_vmem, in_vmem, in_hbm],
        out_specs=(in_hbm, in_vmem),
        scratch_shapes=[
            pltpu.VMEM((tok_rows, head), jnp.bfloat16),
            pltpu.VMEM((tok_rows, local_width), jnp.bfloat16),
            pltpu.VMEM((ny, nx, nz * rows, width), jnp.bfloat16),
            pltpu.SemaphoreType.DMA((ny + 1,)),
        ],
    )(both, hidden, grad_out_hbm)

    received = lax.all_to_all(sent.reshape(ny * nx, nz * rows, width), NEAR, 0, 0)
    folded = call(
        functools.partial(fold_kernel, rows),
        array((nz * blocks * rows, LANES)),
        300_000_000,
        2_000_000,
    )(received)
    folded = lax.all_to_all(folded.reshape(nz, blocks * rows, LANES), "z", 0, 0)
    own = lax.axis_index(FSDP) * rows
    own_gain = lax.dynamic_slice(gain, (own,), (rows,)).reshape(rows, 1)
    grad_qkv, grad_outw_t, grad_gain = call(
        finish_kernel,
        (
            array((rows, cut), jnp.float32),
            array((rows, head), jnp.float32),
            array((rows, 1), jnp.float32),
        ),
        10_000_000,
        300_000,
    )(folded, qkv_weight, own_gain)

    grad_hidden = lax.dot_general(
        grad_proj, weights[:, :cut], nt_dims, preferred_element_type=jnp.float32
    )
    proj_grad = grad_proj.astype(jnp.float32)
    first = jnp.sum(proj_grad * weight_sums[None, :], axis=1) / model_width
    second = jnp.sum(proj_grad * both[:, :cut].astype(jnp.float32), axis=1) / model_width
    grad_normed = grad_hidden * gain[None, :]
    grad_tokens = grad_out.astype(jnp.float32) + inv_std[:, None] * (
        grad_normed - first[:, None] - normed * second[:, None]
    )
    return (
        grad_tokens.astype(jnp.bfloat16),
        grad_qkv,
        grad_outw_t.T,
        grad_gain.reshape(rows),
    )


def solution(mesh):
    fine = Mesh(mesh.devices.reshape(2, 2, 4, 16, 2), SEC + FSDP)
    placed = (
        P(FSDP, SEC),
        P(FSDP, SEC),
        P(SEC),
        P(SEC + FSDP, None),
        P(None, SEC + FSDP),
    )
    return jax.shard_map(
        on_device,
        mesh=fine,
        in_specs=placed,
        out_specs=(
            P(FSDP, SEC),
            P(SEC + FSDP, None),
            P(None, SEC + FSDP),
            P(SEC + FSDP),
        ),
        check_vma=False,
    )
```

```python
import functools

import jax
import jax.numpy as jnp
from jax import lax
from jax.experimental import pallas as pl
from jax.experimental.pallas import tpu as pltpu
from jax.sharding import Mesh
from jax.sharding import PartitionSpec as P

PATCHES = 256


EPS = 1e-06

SEC = ("xlo", "core")
FSDP = ("y", "z", "xhi")
NEAR = ("xhi", "y")
LANES = 128
VMEM_LIMIT = 28 * 1024 * 1024

nt_dims = (((1,), (1,)), ((), ()))
tn_dims = (((0,), (0,)), ((), ()))


def dot(a, b, dims=(((1,), (0,)), ((), ()))):
    return lax.dot_general(a, b, dims, preferred_element_type=jnp.float32)


def by_rows(index, rows):
    return lax.shift_right_logical(index * (65536 // rows + 1), jnp.full_like(index, 16))


def picks(shape, source_of_row):
    row = lax.broadcasted_iota(jnp.int32, shape, 0)
    column = lax.broadcasted_iota(jnp.int32, shape, 1)
    return (column == source_of_row(row)).astype(jnp.float32).astype(jnp.bfloat16)


def unpack_block(rows, blocks, column_block):
    return lambda i: i + by_rows(i, rows) * (rows * (blocks - 1)) + column_block * rows


def near_order(rows, nz):
    def source(i):
        z = by_rows(i, 2 * rows)
        rest = i - z * 2 * rows
        high = (rest >= rows).astype(jnp.int32)
        return high * (nz * rows) + z * rows + rest - high * rows

    return source


def pack_kernel(qkv_hbm, out_t_hbm, o_ref, qkv_ref, out_t_ref, sem):
    fetches = [
        pltpu.make_async_copy(qkv_hbm, qkv_ref, sem.at[0]),
        pltpu.make_async_copy(out_t_hbm, out_t_ref, sem.at[1]),
    ]
    for fetch in fetches:
        fetch.start()
    for fetch in fetches:
        fetch.wait()
    copies, span, _ = o_ref.shape
    rows = qkv_ref.shape[0]
    blocks = span // rows
    packed = jnp.zeros((span, LANES), jnp.float32)
    for b in range(blocks):
        pick = picks((span, rows), lambda i: i - b * rows)
        last = b == blocks - 1
        block = out_t_ref[...] if last else qkv_ref[:, b * LANES : (b + 1) * LANES]
        packed = packed + dot(pick, block)
    packed = packed.astype(jnp.bfloat16)
    for k in range(copies):
        o_ref[k] = packed


def spread_kernel(rows, x_ref, o_ref):
    copies, span, width = o_ref.shape
    blocks = width // LANES
    x = x_ref[...]
    for b in range(blocks):
        pick = picks((span, x.shape[0]), unpack_block(rows, blocks, b))
        part = dot(pick, x).astype(jnp.bfloat16)
        for k in range(copies):
            o_ref[k, :, b * LANES : (b + 1) * LANES] = part


def project_kernel(
    rows, nz, near_ref, hidden_ref, gout_hbm, gain_ref, w_ref, partial_ref, gout_ref, sem
):
    fetch = pltpu.make_async_copy(gout_hbm, gout_ref, sem)
    fetch.start()
    nx, ny, part, width = near_ref.shape
    span = nx * part
    cut = width - LANES
    half = hidden_ref.shape[0] // 2
    pick = picks((span, span), near_order(rows, nz))
    sums = jnp.zeros((gain_ref.shape[0], cut), jnp.float32)
    for y in range(ny):
        block = jnp.concatenate([near_ref[x, y] for x in range(nx)], axis=0)
        natural = dot(pick, block).astype(jnp.bfloat16)
        w_ref[y * span : (y + 1) * span, :] = natural
        sums = sums + dot(gain_ref[:, y * span : (y + 1) * span], natural[:, :cut])
    proj = dot(hidden_ref[...], w_ref[:, :cut])
    for h in range(2):
        partial_ref[h, half:, :cut] = sums[:8]
        partial_ref[h, half:, cut:] = jnp.zeros((8, LANES), jnp.float32)
        partial_ref[h, :half, :cut] = proj[h * half : (h + 1) * half]
    fetch.wait()
    att = dot(gout_ref[...], w_ref[:, cut:])
    for h in range(2):
        partial_ref[h, :half, cut:] = att[h * half : (h + 1) * half]


def attend_kernel(
    rows, nz, both_ref, hidden_ref, gout_hbm, near_ref, gproj_ref, att_ref, gout_ref, sem
):
    fetch = pltpu.make_async_copy(gout_hbm, gout_ref, sem)
    fetch.start()
    nx, ny, part, width = near_ref.shape
    span = nx * part
    head = LANES
    scale = 1.0 / head**0.5
    for image in range(both_ref.shape[0] // PATCHES):
        at = slice(image * PATCHES, (image + 1) * PATCHES)
        query = both_ref[at, :head]
        key_in = both_ref[at, head : 2 * head]
        value = both_ref[at, 2 * head : 3 * head]
        grad_att = both_ref[at, 3 * head :]
        scores = dot(query, key_in, nt_dims) * scale
        raised = jnp.exp(scores - jnp.max(scores, axis=1, keepdims=True))
        probs = raised / jnp.sum(raised, axis=1, keepdims=True)
        probs_b = probs.astype(jnp.bfloat16)
        att_ref[at, :] = dot(probs_b, value).astype(jnp.bfloat16)
        grad_prob = dot(grad_att, value, nt_dims)
        inner = jnp.sum(grad_prob * probs, axis=1, keepdims=True)
        grad_score = (probs * (grad_prob - inner) * scale).astype(jnp.bfloat16)
        gproj_ref[at, :head] = dot(grad_score, key_in).astype(jnp.bfloat16)
        gproj_ref[at, head : 2 * head] = dot(grad_score, query, tn_dims).astype(jnp.bfloat16)
        gproj_ref[at, 2 * head :] = dot(probs_b, grad_att, tn_dims).astype(jnp.bfloat16)
    row = lax.broadcasted_iota(jnp.int32, (span, span), 0)
    column = lax.broadcasted_iota(jnp.int32, (span, span), 1)
    pick = (row == near_order(rows, nz)(column)).astype(jnp.float32).astype(jnp.bfloat16)
    cut = width - head
    fetch.wait()
    for y in range(ny):
        at = slice(y * span, (y + 1) * span)
        qkv_t = dot(gproj_ref[...], hidden_ref[:, at], tn_dims).astype(jnp.bfloat16)
        out_t = dot(att_ref[...], gout_ref[:, at], tn_dims).astype(jnp.bfloat16)
        sent = dot(pick, qkv_t, nt_dims).astype(jnp.bfloat16)
        for x in range(nx):
            near_ref[x, y, :, :cut] = sent[x * part : (x + 1) * part]
        sent = dot(pick, out_t, nt_dims).astype(jnp.bfloat16)
        for x in range(nx):
            near_ref[x, y, :, cut:] = sent[x * part : (x + 1) * part]


def fold_kernel(rows, near_ref, o_ref):
    copies, span, width = near_ref.shape
    blocks = width // LANES
    total = near_ref[0].astype(jnp.float32)
    for k in range(1, copies):
        total = total + near_ref[k].astype(jnp.float32)
    total = total.astype(jnp.bfloat16)
    row = lax.broadcasted_iota(jnp.int32, (o_ref.shape[0], span), 0)
    column = lax.broadcasted_iota(jnp.int32, (o_ref.shape[0], span), 1)
    packed = jnp.zeros(o_ref.shape, jnp.float32)
    for b in range(blocks):
        pick = row == unpack_block(rows, blocks, b)(column)
        pick = pick.astype(jnp.float32).astype(jnp.bfloat16)
        packed = packed + dot(pick, total[:, b * LANES : (b + 1) * LANES])
    o_ref[...] = packed.astype(jnp.bfloat16)


def finish_kernel(x_ref, qkv_ref, gain_ref, grad_ref, out_t_ref, gg_ref):
    rows = qkv_ref.shape[0]
    copies, span, _ = x_ref.shape
    x = x_ref[...].reshape(copies * span, LANES)
    blocks = span // rows
    row = lax.broadcasted_iota(jnp.int32, (rows, copies * span), 0)
    column = lax.broadcasted_iota(jnp.int32, (rows, copies * span), 1)
    within = column - by_rows(column, span) * span
    products = jnp.zeros((rows, LANES), jnp.float32)
    for b in range(blocks):
        pick = (within == row + b * rows).astype(jnp.float32).astype(jnp.bfloat16)
        part = dot(pick, x)
        if b == blocks - 1:
            out_t_ref[...] = part
        else:
            at = slice(b * LANES, (b + 1) * LANES)
            grad_ref[:, at] = part
            products = products + part * qkv_ref[:, at].astype(jnp.float32)
    ones = jnp.ones((8, LANES), jnp.float32)
    totals = lax.dot_general(
        ones,
        products,
        nt_dims,
        precision=lax.Precision.HIGHEST,
        preferred_element_type=jnp.float32,
    )
    gg_ref[...] = totals[:1] / gain_ref[...]


def call(kernel, out_shape, flops, moved, **more):
    return pl.pallas_call(
        kernel,
        out_shape=out_shape,
        compiler_params=pltpu.CompilerParams(vmem_limit_bytes=VMEM_LIMIT),
        cost_estimate=pl.CostEstimate(flops=flops, bytes_accessed=moved, transcendentals=0),
        **more,
    )


def array(shape, dtype=jnp.bfloat16):
    return jax.ShapeDtypeStruct(shape, dtype)


def on_device(tokens, grad_out, gain, qkv_weight, out_weight):
    tok_rows, local_width = tokens.shape
    model_width = local_width * lax.axis_size(SEC)
    head = out_weight.shape[0]
    rows = qkv_weight.shape[0]
    ny, nz, nx = (lax.axis_size(a) for a in FSDP)
    cut = 3 * head
    width = cut + head
    blocks = width // LANES

    in_hbm = pl.BlockSpec(memory_space=pltpu.HBM)
    in_vmem = pl.BlockSpec(memory_space=pltpu.VMEM)

    def keep(x):
        return pltpu.with_memory_space_constraint(x, pltpu.HBM)

    packed = call(
        pack_kernel,
        array((nz, blocks * rows, LANES)),
        1_000_000,
        200_000,
        in_specs=[in_hbm, in_hbm],
        scratch_shapes=[
            pltpu.VMEM((rows, cut), jnp.bfloat16),
            pltpu.VMEM((rows, head), jnp.bfloat16),
            pltpu.SemaphoreType.DMA((2,)),
        ],
    )(keep(qkv_weight), keep(out_weight.T))
    along_z = lax.all_to_all(packed, "z", 0, 0).reshape(nz * blocks * rows, LANES)

    tok_float = tokens.astype(jnp.float32)
    stats = lax.psum(
        jnp.stack([jnp.sum(tok_float, axis=1), jnp.sum(tok_float * tok_float, axis=1)]), SEC
    )

    row_mean = stats[0] / model_width
    inv_std = lax.rsqrt(stats[1] / model_width - row_mean * row_mean + EPS)
    normed = (tok_float - row_mean[:, None]) * inv_std[:, None]
    hidden = (normed * gain[None, :]).astype(jnp.bfloat16)
    gain_high = gain.astype(jnp.bfloat16)
    gain_low = (gain - gain_high.astype(jnp.float32)).astype(jnp.bfloat16)
    gains = jnp.concatenate(
        [gain_high[None], gain_low[None], jnp.zeros((14, local_width), jnp.bfloat16)], axis=0
    )
    own = lax.axis_index(FSDP) * rows
    own_gain = lax.dynamic_slice(gain, (own,), (rows,)).reshape(1, rows)

    along_z, hidden, gains, own_gain = lax.optimization_barrier(
        (along_z, hidden, gains, own_gain)
    )
    spread = call(
        functools.partial(spread_kernel, rows),
        array((nx * ny, nz * rows, width)),
        300_000_000,
        2_000_000,
    )(along_z)
    near = lax.all_to_all(spread, NEAR, 0, 0)

    grad_out_hbm = keep(grad_out)
    half_rows = tok_rows // 2
    weights, partial = call(
        functools.partial(project_kernel, rows, nz),
        (array((local_width, width)), array((2, half_rows + 8, width), jnp.float32)),
        1_500_000_000,
        8_000_000,
        in_specs=[in_vmem, in_vmem, in_hbm, in_vmem],
        scratch_shapes=[
            pltpu.VMEM((tok_rows, local_width), jnp.bfloat16),
            pltpu.SemaphoreType.DMA,
        ],
    )(near.reshape(nx, ny, nz * rows, width), hidden, grad_out_hbm, gains)

    half = lax.all_to_all(partial, "core", 0, 0)
    half = half[0] + half[1]
    half = half + lax.ppermute(half, "xlo", [(0, 1), (1, 0)])
    weight_sums = half[half_rows, :cut] + half[half_rows + 1, :cut]
    both = lax.all_gather(half[:half_rows].astype(jnp.bfloat16), "core", axis=0, tiled=True)

    both, weight_sums = lax.optimization_barrier((both, weight_sums))
    sent, grad_proj = call(
        functools.partial(attend_kernel, rows, nz),
        (array((nx, ny, nz * rows, width)), array((tok_rows, cut))),
        1_800_000_000,
        6_000_000,
        in_specs=[in_vmem, in_vmem, in_hbm],
        scratch_shapes=[
            pltpu.VMEM((tok_rows, head), jnp.bfloat16),
            pltpu.VMEM((tok_rows, local_width), jnp.bfloat16),
            pltpu.SemaphoreType.DMA,
        ],
    )(both, hidden, grad_out_hbm)

    received = lax.all_to_all(sent.reshape(nx * ny, nz * rows, width), NEAR, 0, 0)
    received, grad_proj = lax.optimization_barrier((received, grad_proj))
    folded = call(
        functools.partial(fold_kernel, rows),
        array((nz * blocks * rows, LANES)),
        300_000_000,
        2_000_000,
    )(received)
    folded = lax.all_to_all(folded.reshape(nz, blocks * rows, LANES), "z", 0, 0)
    grad_qkv, grad_outw_t, grad_gain = call(
        finish_kernel,
        (
            array((rows, cut), jnp.float32),
            array((rows, head), jnp.float32),
            array((1, rows), jnp.float32),
        ),
        10_000_000,
        300_000,
    )(folded, qkv_weight, own_gain)

    grad_hidden = lax.dot_general(
        grad_proj, weights[:, :cut], nt_dims, preferred_element_type=jnp.float32
    )
    proj_grad = grad_proj.astype(jnp.float32)
    first = jnp.sum(proj_grad * weight_sums[None, :], axis=1) / model_width
    second = jnp.sum(proj_grad * both[:, :cut].astype(jnp.float32), axis=1) / model_width
    grad_normed = grad_hidden * gain[None, :]
    grad_tokens = grad_out.astype(jnp.float32) + inv_std[:, None] * (
        grad_normed - first[:, None] - normed * second[:, None]
    )
    return (
        grad_tokens.astype(jnp.bfloat16),
        grad_qkv,
        grad_outw_t.T,
        grad_gain.reshape(rows),
    )


def solution(mesh):
    fine = Mesh(mesh.devices.reshape(2, 2, 4, 16, 2), SEC + FSDP)
    placed = (
        P(FSDP, SEC),
        P(FSDP, SEC),
        P(SEC),
        P(SEC + FSDP, None),
        P(None, SEC + FSDP),
    )
    return jax.shard_map(
        on_device,
        mesh=fine,
        in_specs=placed,
        out_specs=(
            P(FSDP, SEC),
            P(SEC + FSDP, None),
            P(None, SEC + FSDP),
            P(SEC + FSDP),
        ),
        check_vma=False,
    )
```

```python
import functools

import jax
import jax.numpy as jnp
from jax import lax
from jax.experimental import pallas as pl
from jax.experimental.pallas import tpu as pltpu
from jax.sharding import Mesh
from jax.sharding import PartitionSpec as P

PATCHES = 256


EPS = 1e-06

SEC = ("xlo", "core")
FSDP = ("y", "z", "xhi")
NEAR = ("xhi", "y")
LANES = 128
VMEM_LIMIT = 28 * 1024 * 1024

nt_dims = (((1,), (1,)), ((), ()))
tn_dims = (((0,), (0,)), ((), ()))


def dot(a, b, dims=(((1,), (0,)), ((), ()))):
    return lax.dot_general(a, b, dims, preferred_element_type=jnp.float32)


def by_rows(index, rows):
    return lax.shift_right_logical(index * (65536 // rows + 1), jnp.full_like(index, 16))


def picks(shape, source_of_row):
    row = lax.broadcasted_iota(jnp.int32, shape, 0)
    column = lax.broadcasted_iota(jnp.int32, shape, 1)
    return (column == source_of_row(row)).astype(jnp.float32).astype(jnp.bfloat16)


def unpack_block(rows, blocks, column_block):
    return lambda i: i + by_rows(i, rows) * (rows * (blocks - 1)) + column_block * rows


def near_order(rows, nz):
    def source(i):
        z = by_rows(i, 2 * rows)
        rest = i - z * 2 * rows
        high = (rest >= rows).astype(jnp.int32)
        return high * (nz * rows) + z * rows + rest - high * rows

    return source


def pack_kernel(qkv_hbm, out_t_hbm, o_ref, qkv_ref, out_t_ref, sem):
    fetches = [
        pltpu.make_async_copy(qkv_hbm, qkv_ref, sem.at[0]),
        pltpu.make_async_copy(out_t_hbm, out_t_ref, sem.at[1]),
    ]
    for fetch in fetches:
        fetch.start()
    for fetch in fetches:
        fetch.wait()
    copies, span, _ = o_ref.shape
    rows = qkv_ref.shape[0]
    blocks = span // rows
    packed = jnp.zeros((span, LANES), jnp.float32)
    for b in range(blocks):
        pick = picks((span, rows), lambda i: i - b * rows)
        last = b == blocks - 1
        block = out_t_ref[...] if last else qkv_ref[:, b * LANES : (b + 1) * LANES]
        packed = packed + dot(pick, block)
    packed = packed.astype(jnp.bfloat16)
    for k in range(copies):
        o_ref[k] = packed


def spread_kernel(rows, x_ref, o_ref):
    copies, span, width = o_ref.shape
    blocks = width // LANES
    x = x_ref[...]
    for b in range(blocks):
        pick = picks((span, x.shape[0]), unpack_block(rows, blocks, b))
        part = dot(pick, x).astype(jnp.bfloat16)
        for k in range(copies):
            o_ref[k, :, b * LANES : (b + 1) * LANES] = part


def prepare_kernel(
    rows, nz, hidden_ref, gout_hbm, gain_ref, hp_ref, gp_ref, gains_ref, gout_ref, sem
):
    fetch = pltpu.make_async_copy(gout_hbm, gout_ref, sem)
    fetch.start()
    span = 2 * nz * rows
    pick = picks((span, span), near_order(rows, nz))
    for y in range(hidden_ref.shape[1] // span):
        at = slice(y * span, (y + 1) * span)
        hp_ref[:, at] = dot(hidden_ref[:, at], pick).astype(jnp.bfloat16)
        gain = gain_ref[:, at]
        high = gain.astype(jnp.bfloat16).astype(jnp.float32)
        row = lax.broadcasted_iota(jnp.int32, (16, span), 0)
        both = jnp.where(row == 0, high, jnp.where(row == 1, gain - high, 0.0))
        gains_ref[:, at] = dot(both.astype(jnp.bfloat16), pick).astype(jnp.bfloat16)
    fetch.wait()
    for y in range(hidden_ref.shape[1] // span):
        at = slice(y * span, (y + 1) * span)
        gp_ref[:, at] = dot(gout_ref[:, at], pick).astype(jnp.bfloat16)


def project_kernel(near_ref, hidden_ref, gout_ref, gain_ref, partial_ref, w_ref):
    nx, ny, part, width = near_ref.shape
    cut = width - LANES
    half = hidden_ref.shape[0] // 2
    for y in range(ny):
        for x in range(nx):
            at = (y * nx + x) * part
            w_ref[at : at + part, :] = near_ref[x, y]
    sums = dot(gain_ref[...], w_ref[:, :cut])
    proj = dot(hidden_ref[...], w_ref[:, :cut])
    att = dot(gout_ref[...], w_ref[:, cut:])
    for h in range(2):
        partial_ref[h, half:, :cut] = sums[:8]
        partial_ref[h, half:, cut:] = jnp.zeros((8, LANES), jnp.float32)
        partial_ref[h, :half, :cut] = proj[h * half : (h + 1) * half]
        partial_ref[h, :half, cut:] = att[h * half : (h + 1) * half]


def natural_kernel(rows, nz, near_ref, o_ref):
    nx, ny, part, _ = near_ref.shape
    span = nx * part
    cut = o_ref.shape[1]
    pick = picks((span, span), near_order(rows, nz))
    for y in range(ny):
        block = jnp.concatenate([near_ref[x, y, :, :cut] for x in range(nx)], axis=0)
        o_ref[y * span : (y + 1) * span, :] = dot(pick, block).astype(jnp.bfloat16)


def add_kernel(own_ref, other_ref, both_ref, sums_ref):
    count = both_ref.shape[0]
    both_ref[...] = (own_ref[:count] + other_ref[:count]).astype(jnp.bfloat16)
    cut = sums_ref.shape[1]
    tail = own_ref[count:, :cut] + other_ref[count:, :cut]
    sums_ref[...] = tail[0:1] + tail[1:2]


def attend_kernel(both_ref, hidden_ref, gout_ref, near_ref, gproj_ref, att_ref):
    nx, ny, part, width = near_ref.shape
    span = nx * part
    head = LANES
    scale = 1.0 / head**0.5
    for image in range(both_ref.shape[0] // PATCHES):
        at = slice(image * PATCHES, (image + 1) * PATCHES)
        query = both_ref[at, :head]
        key_in = both_ref[at, head : 2 * head]
        value = both_ref[at, 2 * head : 3 * head]
        grad_att = both_ref[at, 3 * head :]
        scores = dot(query, key_in, nt_dims) * scale
        raised = jnp.exp(scores - jnp.max(scores, axis=1, keepdims=True))
        probs = raised / jnp.sum(raised, axis=1, keepdims=True)
        probs_b = probs.astype(jnp.bfloat16)
        att_ref[at, :] = dot(probs_b, value).astype(jnp.bfloat16)
        grad_prob = dot(grad_att, value, nt_dims)
        inner = jnp.sum(grad_prob * probs, axis=1, keepdims=True)
        grad_score = (probs * (grad_prob - inner) * scale).astype(jnp.bfloat16)
        gproj_ref[at, :head] = dot(grad_score, key_in).astype(jnp.bfloat16)
        gproj_ref[at, head : 2 * head] = dot(grad_score, query, tn_dims).astype(jnp.bfloat16)
        gproj_ref[at, 2 * head :] = dot(probs_b, grad_att, tn_dims).astype(jnp.bfloat16)
    cut = width - head
    for y in range(ny):
        at = slice(y * span, (y + 1) * span)
        part_qkv = dot(hidden_ref[:, at], gproj_ref[...], tn_dims).astype(jnp.bfloat16)
        part_out = dot(gout_ref[:, at], att_ref[...], tn_dims).astype(jnp.bfloat16)
        for x in range(nx):
            near_ref[x, y, :, :cut] = part_qkv[x * part : (x + 1) * part]
            near_ref[x, y, :, cut:] = part_out[x * part : (x + 1) * part]


def fold_kernel(rows, near_ref, o_ref):
    copies, span, width = near_ref.shape
    blocks = width // LANES
    total = near_ref[0].astype(jnp.float32)
    for k in range(1, copies):
        total = total + near_ref[k].astype(jnp.float32)
    total = total.astype(jnp.bfloat16)
    row = lax.broadcasted_iota(jnp.int32, (o_ref.shape[0], span), 0)
    column = lax.broadcasted_iota(jnp.int32, (o_ref.shape[0], span), 1)
    packed = jnp.zeros(o_ref.shape, jnp.float32)
    for b in range(blocks):
        pick = row == unpack_block(rows, blocks, b)(column)
        pick = pick.astype(jnp.float32).astype(jnp.bfloat16)
        packed = packed + dot(pick, total[:, b * LANES : (b + 1) * LANES])
    o_ref[...] = packed.astype(jnp.bfloat16)


def finish_kernel(x_ref, qkv_ref, gain_ref, grad_ref, out_t_ref, gg_ref):
    rows = qkv_ref.shape[0]
    copies, span, _ = x_ref.shape
    x = x_ref[...].reshape(copies * span, LANES)
    blocks = span // rows
    row = lax.broadcasted_iota(jnp.int32, (rows, copies * span), 0)
    column = lax.broadcasted_iota(jnp.int32, (rows, copies * span), 1)
    within = column - by_rows(column, span) * span
    products = jnp.zeros((rows, LANES), jnp.float32)
    for b in range(blocks):
        pick = (within == row + b * rows).astype(jnp.float32).astype(jnp.bfloat16)
        part = dot(pick, x)
        if b == blocks - 1:
            out_t_ref[...] = part
        else:
            at = slice(b * LANES, (b + 1) * LANES)
            grad_ref[:, at] = part
            products = products + part * qkv_ref[:, at].astype(jnp.float32)
    ones = jnp.ones((8, LANES), jnp.float32)
    totals = lax.dot_general(
        ones,
        products,
        nt_dims,
        precision=lax.Precision.HIGHEST,
        preferred_element_type=jnp.float32,
    )
    gg_ref[...] = totals[:1] / gain_ref[...]


def call(kernel, out_shape, flops, moved, **more):
    return pl.pallas_call(
        kernel,
        out_shape=out_shape,
        compiler_params=pltpu.CompilerParams(vmem_limit_bytes=VMEM_LIMIT),
        cost_estimate=pl.CostEstimate(flops=flops, bytes_accessed=moved, transcendentals=0),
        **more,
    )


def array(shape, dtype=jnp.bfloat16):
    return jax.ShapeDtypeStruct(shape, dtype)


def on_device(tokens, grad_out, gain, qkv_weight, out_weight):
    tok_rows, local_width = tokens.shape
    model_width = local_width * lax.axis_size(SEC)
    head = out_weight.shape[0]
    rows = qkv_weight.shape[0]
    ny, nz, nx = (lax.axis_size(a) for a in FSDP)
    cut = 3 * head
    width = cut + head
    blocks = width // LANES

    in_hbm = pl.BlockSpec(memory_space=pltpu.HBM)
    in_vmem = pl.BlockSpec(memory_space=pltpu.VMEM)

    def keep(x):
        return pltpu.with_memory_space_constraint(x, pltpu.HBM)

    packed = call(
        pack_kernel,
        array((nz, blocks * rows, LANES)),
        1_000_000,
        200_000,
        in_specs=[in_hbm, in_hbm],
        scratch_shapes=[
            pltpu.VMEM((rows, cut), jnp.bfloat16),
            pltpu.VMEM((rows, head), jnp.bfloat16),
            pltpu.SemaphoreType.DMA((2,)),
        ],
    )(keep(qkv_weight), keep(out_weight.T))
    along_z = lax.all_to_all(packed, "z", 0, 0).reshape(nz * blocks * rows, LANES)

    tok_float = tokens.astype(jnp.float32)
    stats = lax.psum(
        jnp.stack([jnp.sum(tok_float, axis=1), jnp.sum(tok_float * tok_float, axis=1)]), SEC
    )

    row_mean = stats[0] / model_width
    inv_std = lax.rsqrt(stats[1] / model_width - row_mean * row_mean + EPS)
    normed = (tok_float - row_mean[:, None]) * inv_std[:, None]
    hidden = (normed * gain[None, :]).astype(jnp.bfloat16)
    hidden_p, gout_p, gains_p = call(
        functools.partial(prepare_kernel, rows, nz),
        (
            array((tok_rows, local_width)),
            array((tok_rows, local_width)),
            array((16, local_width)),
        ),
        1_300_000_000,
        6_000_000,
        in_specs=[in_vmem, in_hbm, in_vmem],
        scratch_shapes=[
            pltpu.VMEM((tok_rows, local_width), jnp.bfloat16),
            pltpu.SemaphoreType.DMA,
        ],
    )(hidden, keep(grad_out), gain.reshape(1, local_width))
    own = lax.axis_index(FSDP) * rows
    own_gain = lax.dynamic_slice(gain, (own,), (rows,)).reshape(1, rows)

    along_z, hidden_p, gout_p, gains_p, own_gain = lax.optimization_barrier(
        (along_z, hidden_p, gout_p, gains_p, own_gain)
    )
    spread = call(
        functools.partial(spread_kernel, rows),
        array((nx * ny, nz * rows, width)),
        300_000_000,
        2_000_000,
    )(along_z)
    near = lax.all_to_all(spread, NEAR, 0, 0)

    near = near.reshape(nx, ny, nz * rows, width)
    half_rows = tok_rows // 2
    partial = call(
        project_kernel,
        array((2, half_rows + 8, width), jnp.float32),
        900_000_000,
        6_000_000,
        scratch_shapes=[pltpu.VMEM((local_width, width), jnp.bfloat16)],
    )(near, hidden_p, gout_p, gains_p)

    near, partial = lax.optimization_barrier((near, partial))
    half = lax.all_to_all(partial, "core", 0, 0)
    half = half[0] + half[1]
    near, half = lax.optimization_barrier((near, half))
    other = lax.ppermute(half, "xlo", [(0, 1), (1, 0)])
    weights = call(
        functools.partial(natural_kernel, rows, nz),
        array((local_width, cut)),
        460_000_000,
        3_000_000,
    )(near)
    half, weight_sums = call(
        add_kernel,
        (array((half_rows, width)), array((1, cut), jnp.float32)),
        300_000,
        1_400_000,
    )(half, other)
    both = lax.all_gather(half, "core", axis=0, tiled=True)

    both, weights = lax.optimization_barrier((both, weights))
    sent, grad_proj = call(
        attend_kernel,
        (array((nx, ny, nz * rows, width)), array((tok_rows, cut))),
        1_300_000_000,
        6_000_000,
        scratch_shapes=[pltpu.VMEM((tok_rows, head), jnp.bfloat16)],
    )(both, hidden_p, gout_p)

    received = lax.all_to_all(sent.reshape(nx * ny, nz * rows, width), NEAR, 0, 0)
    received, grad_proj, weight_sums = lax.optimization_barrier(
        (received, grad_proj, weight_sums)
    )
    folded = call(
        functools.partial(fold_kernel, rows),
        array((nz * blocks * rows, LANES)),
        300_000_000,
        2_000_000,
    )(received)
    folded = lax.all_to_all(folded.reshape(nz, blocks * rows, LANES), "z", 0, 0)
    grad_qkv, grad_outw_t, grad_gain = call(
        finish_kernel,
        (
            array((rows, cut), jnp.float32),
            array((rows, head), jnp.float32),
            array((1, rows), jnp.float32),
        ),
        10_000_000,
        300_000,
    )(folded, qkv_weight, own_gain)

    grad_hidden = lax.dot_general(
        grad_proj, weights, nt_dims, preferred_element_type=jnp.float32
    )
    proj_grad = grad_proj.astype(jnp.float32)
    first = jnp.sum(proj_grad * weight_sums, axis=1) / model_width
    second = jnp.sum(proj_grad * both[:, :cut].astype(jnp.float32), axis=1) / model_width
    grad_normed = grad_hidden * gain[None, :]
    grad_tokens = grad_out.astype(jnp.float32) + inv_std[:, None] * (
        grad_normed - first[:, None] - normed * second[:, None]
    )
    return (
        grad_tokens.astype(jnp.bfloat16),
        grad_qkv,
        grad_outw_t.T,
        grad_gain.reshape(rows),
    )


def solution(mesh):
    fine = Mesh(mesh.devices.reshape(2, 2, 4, 16, 2), SEC + FSDP)
    placed = (
        P(FSDP, SEC),
        P(FSDP, SEC),
        P(SEC),
        P(SEC + FSDP, None),
        P(None, SEC + FSDP),
    )
    return jax.shard_map(
        on_device,
        mesh=fine,
        in_specs=placed,
        out_specs=(
            P(FSDP, SEC),
            P(SEC + FSDP, None),
            P(None, SEC + FSDP),
            P(SEC + FSDP),
        ),
        check_vma=False,
    )
```

```python
import functools

import jax
import jax.numpy as jnp
from jax import lax
from jax.experimental import pallas as pl
from jax.experimental.pallas import tpu as pltpu
from jax.sharding import Mesh
from jax.sharding import PartitionSpec as P

PATCHES = 256


EPS = 1e-06

SEC = ("xlo", "core")
FSDP = ("y", "z", "xhi")
NEAR = ("core", "y", "xhi")
FAR = ("core", "z")
LANES = 128
VMEM_LIMIT = 28 * 1024 * 1024

nt_dims = (((1,), (1,)), ((), ()))
tn_dims = (((0,), (0,)), ((), ()))


def dot(a, b, dims=(((1,), (0,)), ((), ()))):
    return lax.dot_general(a, b, dims, preferred_element_type=jnp.float32)


def by_rows(index, rows):
    return lax.shift_right_logical(index * (65536 // rows + 1), jnp.full_like(index, 16))


def picks(shape, source_of_row):
    row = lax.broadcasted_iota(jnp.int32, shape, 0)
    column = lax.broadcasted_iota(jnp.int32, shape, 1)
    return (column == source_of_row(row)).astype(jnp.float32).astype(jnp.bfloat16)


def mirrored(index, count):
    return index + lax.axis_index("core") * (count - 1 - 2 * index)


def near_all_to_all(x):
    ny, nx = lax.axis_size("y"), lax.axis_size("xhi")
    groups = [
        [(c * ny + (y if c == 0 else ny - 1 - y)) * nx + h for h in range(nx) for y in range(ny)]
        for c in range(2)
    ]
    return lax.all_to_all(x, NEAR, 0, 0, axis_index_groups=groups)


def far_all_to_all(x):
    nz = lax.axis_size("z")
    groups = [list(range(nz)), list(range(2 * nz - 1, nz - 1, -1))]
    return lax.all_to_all(x, FAR, 0, 0, axis_index_groups=groups)


def unpack_block(rows, blocks, column_block, nz):
    def source(i):
        z = by_rows(i, rows)
        return mirrored(z, nz) * (rows * blocks) + column_block * rows + i - z * rows

    return source


def near_order(rows, nz):
    def source(i):
        z = by_rows(i, 2 * rows)
        rest = i - z * 2 * rows
        high = (rest >= rows).astype(jnp.int32)
        return high * (nz * rows) + z * rows + rest - high * rows

    return source


def pack_kernel(qkv_hbm, out_t_hbm, o_ref, qkv_ref, out_t_ref, sem):
    fetches = [
        pltpu.make_async_copy(qkv_hbm, qkv_ref, sem.at[0]),
        pltpu.make_async_copy(out_t_hbm, out_t_ref, sem.at[1]),
    ]
    for fetch in fetches:
        fetch.start()
    for fetch in fetches:
        fetch.wait()
    copies, span, _ = o_ref.shape
    rows = qkv_ref.shape[0]
    blocks = span // rows
    packed = jnp.zeros((span, LANES), jnp.float32)
    for b in range(blocks):
        pick = picks((span, rows), lambda i: i - b * rows)
        last = b == blocks - 1
        block = out_t_ref[...] if last else qkv_ref[:, b * LANES : (b + 1) * LANES]
        packed = packed + dot(pick, block)
    packed = packed.astype(jnp.bfloat16)
    for k in range(copies):
        o_ref[k] = packed


def spread_kernel(rows, x_ref, o_ref):
    copies, span, width = o_ref.shape
    blocks = width // LANES
    x = x_ref[...]
    for b in range(blocks):
        pick = picks((span, x.shape[0]), unpack_block(rows, blocks, b, span // rows))
        part = dot(pick, x).astype(jnp.bfloat16)
        for k in range(copies):
            o_ref[k, :, b * LANES : (b + 1) * LANES] = part


def prepare_kernel(
    rows, nz, hidden_ref, gout_hbm, gain_ref, hp_ref, gp_ref, gains_ref, gout_ref, sem
):
    fetch = pltpu.make_async_copy(gout_hbm, gout_ref, sem)
    fetch.start()
    span = 2 * nz * rows
    pick = picks((span, span), near_order(rows, nz))
    for y in range(hidden_ref.shape[1] // span):
        at = slice(y * span, (y + 1) * span)
        hp_ref[:, at] = dot(hidden_ref[:, at], pick).astype(jnp.bfloat16)
        gain = gain_ref[:, at]
        high = gain.astype(jnp.bfloat16).astype(jnp.float32)
        row = lax.broadcasted_iota(jnp.int32, (16, span), 0)
        both = jnp.where(row == 0, high, jnp.where(row == 1, gain - high, 0.0))
        gains_ref[:, at] = dot(both.astype(jnp.bfloat16), pick).astype(jnp.bfloat16)
    fetch.wait()
    for y in range(hidden_ref.shape[1] // span):
        at = slice(y * span, (y + 1) * span)
        gp_ref[:, at] = dot(gout_ref[:, at], pick).astype(jnp.bfloat16)


def project_kernel(near_ref, hidden_ref, gout_ref, gain_ref, partial_ref, w_ref):
    nx, ny, part, width = near_ref.shape
    cut = width - LANES
    half = hidden_ref.shape[0] // 2
    for y in range(ny):
        for x in range(nx):
            at = (y * nx + x) * part
            w_ref[at : at + part, :] = near_ref[x, mirrored(y, ny)]
    sums = dot(gain_ref[...], w_ref[:, :cut])
    proj = dot(hidden_ref[...], w_ref[:, :cut])
    att = dot(gout_ref[...], w_ref[:, cut:])
    for h in range(2):
        partial_ref[h, half:, :cut] = sums[:8]
        partial_ref[h, half:, cut:] = jnp.zeros((8, LANES), jnp.float32)
        partial_ref[h, :half, :cut] = proj[h * half : (h + 1) * half]
        partial_ref[h, :half, cut:] = att[h * half : (h + 1) * half]


def natural_kernel(rows, nz, near_ref, o_ref):
    nx, ny, part, _ = near_ref.shape
    span = nx * part
    cut = o_ref.shape[1]
    pick = picks((span, span), near_order(rows, nz))
    for y in range(ny):
        block = jnp.concatenate([near_ref[x, mirrored(y, ny), :, :cut] for x in range(nx)], axis=0)
        o_ref[y * span : (y + 1) * span, :] = dot(pick, block).astype(jnp.bfloat16)


def add_kernel(own_ref, other_ref, both_ref, sums_ref):
    count = both_ref.shape[0]
    both_ref[...] = (own_ref[:count] + other_ref[:count]).astype(jnp.bfloat16)
    cut = sums_ref.shape[1]
    tail = own_ref[count:, :cut] + other_ref[count:, :cut]
    sums_ref[...] = tail[0:1] + tail[1:2]


def attend_kernel(both_ref, hidden_ref, gout_ref, near_ref, gproj_ref, att_ref):
    nx, ny, part, width = near_ref.shape
    span = nx * part
    head = LANES
    scale = 1.0 / head**0.5
    for image in range(both_ref.shape[0] // PATCHES):
        at = slice(image * PATCHES, (image + 1) * PATCHES)
        query = both_ref[at, :head]
        key_in = both_ref[at, head : 2 * head]
        value = both_ref[at, 2 * head : 3 * head]
        grad_att = both_ref[at, 3 * head :]
        scores = dot(query, key_in, nt_dims) * scale
        raised = jnp.exp(scores - jnp.max(scores, axis=1, keepdims=True))
        probs = raised / jnp.sum(raised, axis=1, keepdims=True)
        probs_b = probs.astype(jnp.bfloat16)
        att_ref[at, :] = dot(probs_b, value).astype(jnp.bfloat16)
        grad_prob = dot(grad_att, value, nt_dims)
        inner = jnp.sum(grad_prob * probs, axis=1, keepdims=True)
        grad_score = (probs * (grad_prob - inner) * scale).astype(jnp.bfloat16)
        gproj_ref[at, :head] = dot(grad_score, key_in).astype(jnp.bfloat16)
        gproj_ref[at, head : 2 * head] = dot(grad_score, query, tn_dims).astype(jnp.bfloat16)
        gproj_ref[at, 2 * head :] = dot(probs_b, grad_att, tn_dims).astype(jnp.bfloat16)
    cut = width - head
    for y in range(ny):
        at = slice(y * span, (y + 1) * span)
        part_qkv = dot(hidden_ref[:, at], gproj_ref[...], tn_dims).astype(jnp.bfloat16)
        part_out = dot(gout_ref[:, at], att_ref[...], tn_dims).astype(jnp.bfloat16)
        for x in range(nx):
            listed = mirrored(y, ny)
            near_ref[x, listed, :, :cut] = part_qkv[x * part : (x + 1) * part]
            near_ref[x, listed, :, cut:] = part_out[x * part : (x + 1) * part]


def fold_kernel(rows, near_ref, o_ref):
    copies, span, width = near_ref.shape
    blocks = width // LANES
    total = near_ref[0].astype(jnp.float32)
    for k in range(1, copies):
        total = total + near_ref[k].astype(jnp.float32)
    total = total.astype(jnp.bfloat16)
    row = lax.broadcasted_iota(jnp.int32, (o_ref.shape[0], span), 0)
    column = lax.broadcasted_iota(jnp.int32, (o_ref.shape[0], span), 1)
    packed = jnp.zeros(o_ref.shape, jnp.float32)
    for b in range(blocks):
        pick = row == unpack_block(rows, blocks, b, span // rows)(column)
        pick = pick.astype(jnp.float32).astype(jnp.bfloat16)
        packed = packed + dot(pick, total[:, b * LANES : (b + 1) * LANES])
    o_ref[...] = packed.astype(jnp.bfloat16)


def finish_kernel(x_ref, qkv_ref, gain_ref, grad_ref, out_t_ref, gg_ref):
    rows = qkv_ref.shape[0]
    copies, span, _ = x_ref.shape
    x = x_ref[...].reshape(copies * span, LANES)
    blocks = span // rows
    row = lax.broadcasted_iota(jnp.int32, (rows, copies * span), 0)
    column = lax.broadcasted_iota(jnp.int32, (rows, copies * span), 1)
    within = column - by_rows(column, span) * span
    products = jnp.zeros((rows, LANES), jnp.float32)
    for b in range(blocks):
        pick = (within == row + b * rows).astype(jnp.float32).astype(jnp.bfloat16)
        part = dot(pick, x)
        if b == blocks - 1:
            out_t_ref[...] = part
        else:
            at = slice(b * LANES, (b + 1) * LANES)
            grad_ref[:, at] = part
            products = products + part * qkv_ref[:, at].astype(jnp.float32)
    ones = jnp.ones((8, LANES), jnp.float32)
    totals = lax.dot_general(
        ones,
        products,
        nt_dims,
        precision=lax.Precision.HIGHEST,
        preferred_element_type=jnp.float32,
    )
    gg_ref[...] = totals[:1] / gain_ref[...]


def call(kernel, out_shape, flops, moved, **more):
    return pl.pallas_call(
        kernel,
        out_shape=out_shape,
        compiler_params=pltpu.CompilerParams(vmem_limit_bytes=VMEM_LIMIT),
        cost_estimate=pl.CostEstimate(flops=flops, bytes_accessed=moved, transcendentals=0),
        **more,
    )


def array(shape, dtype=jnp.bfloat16):
    return jax.ShapeDtypeStruct(shape, dtype)


def on_device(tokens, grad_out, gain, qkv_weight, out_weight):
    tok_rows, local_width = tokens.shape
    model_width = local_width * lax.axis_size(SEC)
    head = out_weight.shape[0]
    rows = qkv_weight.shape[0]
    ny, nz, nx = (lax.axis_size(a) for a in FSDP)
    cut = 3 * head
    width = cut + head
    blocks = width // LANES

    in_hbm = pl.BlockSpec(memory_space=pltpu.HBM)
    in_vmem = pl.BlockSpec(memory_space=pltpu.VMEM)

    def keep(x):
        return pltpu.with_memory_space_constraint(x, pltpu.HBM)

    packed = call(
        pack_kernel,
        array((nz, blocks * rows, LANES)),
        1_000_000,
        200_000,
        in_specs=[in_hbm, in_hbm],
        scratch_shapes=[
            pltpu.VMEM((rows, cut), jnp.bfloat16),
            pltpu.VMEM((rows, head), jnp.bfloat16),
            pltpu.SemaphoreType.DMA((2,)),
        ],
    )(keep(qkv_weight), keep(out_weight.T))
    along_z = far_all_to_all(packed).reshape(nz * blocks * rows, LANES)

    tok_float = tokens.astype(jnp.float32)
    stats = lax.psum(
        jnp.stack([jnp.sum(tok_float, axis=1), jnp.sum(tok_float * tok_float, axis=1)]), SEC
    )

    row_mean = stats[0] / model_width
    inv_std = lax.rsqrt(stats[1] / model_width - row_mean * row_mean + EPS)
    normed = (tok_float - row_mean[:, None]) * inv_std[:, None]
    hidden = (normed * gain[None, :]).astype(jnp.bfloat16)
    hidden_p, gout_p, gains_p = call(
        functools.partial(prepare_kernel, rows, nz),
        (
            array((tok_rows, local_width)),
            array((tok_rows, local_width)),
            array((16, local_width)),
        ),
        1_300_000_000,
        6_000_000,
        in_specs=[in_vmem, in_hbm, in_vmem],
        scratch_shapes=[
            pltpu.VMEM((tok_rows, local_width), jnp.bfloat16),
            pltpu.SemaphoreType.DMA,
        ],
    )(hidden, keep(grad_out), gain.reshape(1, local_width))
    own = lax.axis_index(FSDP) * rows
    own_gain = lax.dynamic_slice(gain, (own,), (rows,)).reshape(1, rows)

    along_z, hidden_p, gout_p, gains_p, own_gain = lax.optimization_barrier(
        (along_z, hidden_p, gout_p, gains_p, own_gain)
    )
    spread = call(
        functools.partial(spread_kernel, rows),
        array((nx * ny, nz * rows, width)),
        300_000_000,
        2_000_000,
    )(along_z)
    near = near_all_to_all(spread)

    near = near.reshape(nx, ny, nz * rows, width)
    half_rows = tok_rows // 2
    partial = call(
        project_kernel,
        array((2, half_rows + 8, width), jnp.float32),
        900_000_000,
        6_000_000,
        scratch_shapes=[pltpu.VMEM((local_width, width), jnp.bfloat16)],
    )(near, hidden_p, gout_p, gains_p)

    near, partial = lax.optimization_barrier((near, partial))
    half = lax.all_to_all(partial, "core", 0, 0)
    half = half[0] + half[1]
    near, half = lax.optimization_barrier((near, half))
    other = lax.ppermute(half, "xlo", [(0, 1), (1, 0)])
    weights = call(
        functools.partial(natural_kernel, rows, nz),
        array((local_width, cut)),
        460_000_000,
        3_000_000,
    )(near)
    half, weight_sums = call(
        add_kernel,
        (array((half_rows, width)), array((1, cut), jnp.float32)),
        300_000,
        1_400_000,
    )(half, other)
    both = lax.all_gather(half, "core", axis=0, tiled=True)

    both, weights = lax.optimization_barrier((both, weights))
    sent, grad_proj = call(
        attend_kernel,
        (array((nx, ny, nz * rows, width)), array((tok_rows, cut))),
        1_300_000_000,
        6_000_000,
        scratch_shapes=[pltpu.VMEM((tok_rows, head), jnp.bfloat16)],
    )(both, hidden_p, gout_p)

    received = near_all_to_all(sent.reshape(nx * ny, nz * rows, width))
    received, grad_proj, weight_sums = lax.optimization_barrier(
        (received, grad_proj, weight_sums)
    )
    folded = call(
        functools.partial(fold_kernel, rows),
        array((nz * blocks * rows, LANES)),
        300_000_000,
        2_000_000,
    )(received)
    folded = far_all_to_all(folded.reshape(nz, blocks * rows, LANES))
    grad_qkv, grad_outw_t, grad_gain = call(
        finish_kernel,
        (
            array((rows, cut), jnp.float32),
            array((rows, head), jnp.float32),
            array((1, rows), jnp.float32),
        ),
        10_000_000,
        300_000,
    )(folded, qkv_weight, own_gain)

    grad_hidden = lax.dot_general(
        grad_proj, weights, nt_dims, preferred_element_type=jnp.float32
    )
    proj_grad = grad_proj.astype(jnp.float32)
    first = jnp.sum(proj_grad * weight_sums, axis=1) / model_width
    second = jnp.sum(proj_grad * both[:, :cut].astype(jnp.float32), axis=1) / model_width
    grad_normed = grad_hidden * gain[None, :]
    grad_tokens = grad_out.astype(jnp.float32) + inv_std[:, None] * (
        grad_normed - first[:, None] - normed * second[:, None]
    )
    return (
        grad_tokens.astype(jnp.bfloat16),
        grad_qkv,
        grad_outw_t.T,
        grad_gain.reshape(rows),
    )


def solution(mesh):
    fine = Mesh(mesh.devices.reshape(2, 2, 4, 16, 2), SEC + FSDP)
    placed = (
        P(FSDP, SEC),
        P(FSDP, SEC),
        P(SEC),
        P(SEC + FSDP, None),
        P(None, SEC + FSDP),
    )
    return jax.shard_map(
        on_device,
        mesh=fine,
        in_specs=placed,
        out_specs=(
            P(FSDP, SEC),
            P(SEC + FSDP, None),
            P(None, SEC + FSDP),
            P(SEC + FSDP),
        ),
        check_vma=False,
    )
```

```python
import functools

import jax
import jax.numpy as jnp
from jax import lax
from jax.experimental import pallas as pl
from jax.experimental.pallas import tpu as pltpu
from jax.sharding import Mesh
from jax.sharding import PartitionSpec as P

PATCHES = 256


EPS = 1e-06

SEC = ("xlo", "core")
FSDP = ("y", "z", "xhi")
NEAR = ("core", "y", "xhi")
FAR = ("core", "z")
LANES = 128
VMEM_LIMIT = 28 * 1024 * 1024

nt_dims = (((1,), (1,)), ((), ()))
tn_dims = (((0,), (0,)), ((), ()))


def dot(a, b, dims=(((1,), (0,)), ((), ()))):
    return lax.dot_general(a, b, dims, preferred_element_type=jnp.float32)


def by_rows(index, rows):
    return lax.shift_right_logical(index * (65536 // rows + 1), jnp.full_like(index, 16))


def picks(shape, source_of_row):
    row = lax.broadcasted_iota(jnp.int32, shape, 0)
    column = lax.broadcasted_iota(jnp.int32, shape, 1)
    return (column == source_of_row(row)).astype(jnp.float32).astype(jnp.bfloat16)


def mirrored(index, count):
    return index + lax.axis_index("core") * (count - 1 - 2 * index)


def near_all_to_all(x):
    ny, nx = lax.axis_size("y"), lax.axis_size("xhi")
    groups = [
        [(c * ny + (y if c == 0 else ny - 1 - y)) * nx + h for h in range(nx) for y in range(ny)]
        for c in range(2)
    ]
    return lax.all_to_all(x, NEAR, 0, 0, axis_index_groups=groups)


def far_all_to_all(x):
    nz = lax.axis_size("z")
    groups = [list(range(nz)), list(range(2 * nz - 1, nz - 1, -1))]
    return lax.all_to_all(x, FAR, 0, 0, axis_index_groups=groups)


def unpack_block(rows, blocks, column_block, nz):
    def source(i):
        z = by_rows(i, rows)
        return mirrored(z, nz) * (rows * blocks) + column_block * rows + i - z * rows

    return source


def near_order(rows, nz):
    def source(i):
        z = by_rows(i, 2 * rows)
        rest = i - z * 2 * rows
        high = (rest >= rows).astype(jnp.int32)
        return high * (nz * rows) + z * rows + rest - high * rows

    return source


def pack_kernel(qkv_hbm, out_t_hbm, o_ref, qkv_ref, out_t_ref, sem):
    fetches = [
        pltpu.make_async_copy(qkv_hbm, qkv_ref, sem.at[0]),
        pltpu.make_async_copy(out_t_hbm, out_t_ref, sem.at[1]),
    ]
    for fetch in fetches:
        fetch.start()
    for fetch in fetches:
        fetch.wait()
    copies, span, _ = o_ref.shape
    rows = qkv_ref.shape[0]
    blocks = span // rows
    packed = jnp.zeros((span, LANES), jnp.float32)
    for b in range(blocks):
        pick = picks((span, rows), lambda i: i - b * rows)
        last = b == blocks - 1
        block = out_t_ref[...] if last else qkv_ref[:, b * LANES : (b + 1) * LANES]
        packed = packed + dot(pick, block)
    packed = packed.astype(jnp.bfloat16)
    for k in range(copies):
        o_ref[k] = packed


def spread_kernel(rows, x_ref, o_ref):
    copies, span, width = o_ref.shape
    blocks = width // LANES
    x = x_ref[...]
    for b in range(blocks):
        pick = picks((span, x.shape[0]), unpack_block(rows, blocks, b, span // rows))
        part = dot(pick, x).astype(jnp.bfloat16)
        for k in range(copies):
            o_ref[k, :, b * LANES : (b + 1) * LANES] = part


def prepare_kernel(
    rows, nz, hidden_ref, gout_hbm, gain_ref, hp_hbm, gp_ref, gains_ref, gout_ref, hp_ref, sem
):
    fetch = pltpu.make_async_copy(gout_hbm, gout_ref, sem.at[0])
    fetch.start()
    span = 2 * nz * rows
    pick = picks((span, span), near_order(rows, nz))
    for y in range(hidden_ref.shape[1] // span):
        at = slice(y * span, (y + 1) * span)
        hp_ref[:, at] = dot(hidden_ref[:, at], pick).astype(jnp.bfloat16)
        gain = gain_ref[:, at]
        high = gain.astype(jnp.bfloat16).astype(jnp.float32)
        row = lax.broadcasted_iota(jnp.int32, (16, span), 0)
        both = jnp.where(row == 0, high, jnp.where(row == 1, gain - high, 0.0))
        gains_ref[:, at] = dot(both.astype(jnp.bfloat16), pick).astype(jnp.bfloat16)
    store = pltpu.make_async_copy(hp_ref, hp_hbm, sem.at[1])
    store.start()
    fetch.wait()
    for y in range(hidden_ref.shape[1] // span):
        at = slice(y * span, (y + 1) * span)
        gp_ref[:, at] = dot(gout_ref[:, at], pick).astype(jnp.bfloat16)
    store.wait()


def project_kernel(near_ref, hidden_ref, gout_ref, gain_ref, partial_ref, w_ref):
    nx, ny, part, width = near_ref.shape
    cut = width - LANES
    half = hidden_ref.shape[0] // 2
    for y in range(ny):
        for x in range(nx):
            at = (y * nx + x) * part
            w_ref[at : at + part, :] = near_ref[x, mirrored(y, ny)]
    sums = dot(gain_ref[...], w_ref[:, :cut])
    proj = dot(hidden_ref[...], w_ref[:, :cut])
    att = dot(gout_ref[...], w_ref[:, cut:])
    for h in range(2):
        partial_ref[h, half:, :cut] = sums[:8]
        partial_ref[h, half:, cut:] = jnp.zeros((8, LANES), jnp.float32)
        partial_ref[h, :half, :cut] = proj[h * half : (h + 1) * half]
        partial_ref[h, :half, cut:] = att[h * half : (h + 1) * half]


def natural_kernel(rows, nz, near_ref, o_ref):
    nx, ny, part, _ = near_ref.shape
    span = nx * part
    cut = o_ref.shape[1]
    pick = picks((span, span), near_order(rows, nz))
    for y in range(ny):
        block = jnp.concatenate([near_ref[x, mirrored(y, ny), :, :cut] for x in range(nx)], axis=0)
        o_ref[y * span : (y + 1) * span, :] = dot(pick, block).astype(jnp.bfloat16)


def add_kernel(own_ref, other_ref, both_ref, sums_ref):
    count = both_ref.shape[0]
    both_ref[...] = (own_ref[:count] + other_ref[:count]).astype(jnp.bfloat16)
    cut = sums_ref.shape[1]
    tail = own_ref[count:, :cut] + other_ref[count:, :cut]
    sums_ref[...] = tail[0:1] + tail[1:2]


def attend_kernel(both_ref, hidden_ref, gout_ref, near_ref, gproj_ref, att_ref):
    nx, ny, part, width = near_ref.shape
    span = nx * part
    head = LANES
    scale = 1.0 / head**0.5
    for image in range(both_ref.shape[0] // PATCHES):
        at = slice(image * PATCHES, (image + 1) * PATCHES)
        query = both_ref[at, :head]
        key_in = both_ref[at, head : 2 * head]
        value = both_ref[at, 2 * head : 3 * head]
        grad_att = both_ref[at, 3 * head :]
        scores = dot(query, key_in, nt_dims) * scale
        raised = jnp.exp(scores - jnp.max(scores, axis=1, keepdims=True))
        probs = raised / jnp.sum(raised, axis=1, keepdims=True)
        probs_b = probs.astype(jnp.bfloat16)
        att_ref[at, :] = dot(probs_b, value).astype(jnp.bfloat16)
        grad_prob = dot(grad_att, value, nt_dims)
        inner = jnp.sum(grad_prob * probs, axis=1, keepdims=True)
        grad_score = (probs * (grad_prob - inner) * scale).astype(jnp.bfloat16)
        gproj_ref[at, :head] = dot(grad_score, key_in).astype(jnp.bfloat16)
        gproj_ref[at, head : 2 * head] = dot(grad_score, query, tn_dims).astype(jnp.bfloat16)
        gproj_ref[at, 2 * head :] = dot(probs_b, grad_att, tn_dims).astype(jnp.bfloat16)
    cut = width - head
    for y in range(ny):
        at = slice(y * span, (y + 1) * span)
        part_qkv = dot(hidden_ref[:, at], gproj_ref[...], tn_dims).astype(jnp.bfloat16)
        part_out = dot(gout_ref[:, at], att_ref[...], tn_dims).astype(jnp.bfloat16)
        for x in range(nx):
            listed = mirrored(y, ny)
            near_ref[x, listed, :, :cut] = part_qkv[x * part : (x + 1) * part]
            near_ref[x, listed, :, cut:] = part_out[x * part : (x + 1) * part]


def fold_kernel(rows, near_ref, o_ref):
    copies, span, width = near_ref.shape
    blocks = width // LANES
    total = near_ref[0].astype(jnp.float32)
    for k in range(1, copies):
        total = total + near_ref[k].astype(jnp.float32)
    total = total.astype(jnp.bfloat16)
    row = lax.broadcasted_iota(jnp.int32, (o_ref.shape[0], span), 0)
    column = lax.broadcasted_iota(jnp.int32, (o_ref.shape[0], span), 1)
    packed = jnp.zeros(o_ref.shape, jnp.float32)
    for b in range(blocks):
        pick = row == unpack_block(rows, blocks, b, span // rows)(column)
        pick = pick.astype(jnp.float32).astype(jnp.bfloat16)
        packed = packed + dot(pick, total[:, b * LANES : (b + 1) * LANES])
    o_ref[...] = packed.astype(jnp.bfloat16)


def finish_kernel(x_ref, qkv_ref, gain_ref, grad_ref, out_t_ref, gg_ref):
    rows = qkv_ref.shape[0]
    copies, span, _ = x_ref.shape
    x = x_ref[...].reshape(copies * span, LANES)
    blocks = span // rows
    row = lax.broadcasted_iota(jnp.int32, (rows, copies * span), 0)
    column = lax.broadcasted_iota(jnp.int32, (rows, copies * span), 1)
    within = column - by_rows(column, span) * span
    products = jnp.zeros((rows, LANES), jnp.float32)
    for b in range(blocks):
        pick = (within == row + b * rows).astype(jnp.float32).astype(jnp.bfloat16)
        part = dot(pick, x)
        if b == blocks - 1:
            out_t_ref[...] = part
        else:
            at = slice(b * LANES, (b + 1) * LANES)
            grad_ref[:, at] = part
            products = products + part * qkv_ref[:, at].astype(jnp.float32)
    ones = jnp.ones((8, LANES), jnp.float32)
    totals = lax.dot_general(
        ones,
        products,
        nt_dims,
        precision=lax.Precision.HIGHEST,
        preferred_element_type=jnp.float32,
    )
    gg_ref[...] = totals[:1] / gain_ref[...]


def call(kernel, out_shape, flops, moved, **more):
    return pl.pallas_call(
        kernel,
        out_shape=out_shape,
        compiler_params=pltpu.CompilerParams(vmem_limit_bytes=VMEM_LIMIT),
        cost_estimate=pl.CostEstimate(flops=flops, bytes_accessed=moved, transcendentals=0),
        **more,
    )


def array(shape, dtype=jnp.bfloat16):
    return jax.ShapeDtypeStruct(shape, dtype)


def on_device(tokens, grad_out, gain, qkv_weight, out_weight):
    tok_rows, local_width = tokens.shape
    model_width = local_width * lax.axis_size(SEC)
    head = out_weight.shape[0]
    rows = qkv_weight.shape[0]
    ny, nz, nx = (lax.axis_size(a) for a in FSDP)
    cut = 3 * head
    width = cut + head
    blocks = width // LANES

    in_hbm = pl.BlockSpec(memory_space=pltpu.HBM)
    in_vmem = pl.BlockSpec(memory_space=pltpu.VMEM)

    def keep(x):
        return pltpu.with_memory_space_constraint(x, pltpu.HBM)

    packed = call(
        pack_kernel,
        array((nz, blocks * rows, LANES)),
        1_000_000,
        200_000,
        in_specs=[in_hbm, in_hbm],
        scratch_shapes=[
            pltpu.VMEM((rows, cut), jnp.bfloat16),
            pltpu.VMEM((rows, head), jnp.bfloat16),
            pltpu.SemaphoreType.DMA((2,)),
        ],
    )(keep(qkv_weight), keep(out_weight.T))
    along_z = far_all_to_all(packed).reshape(nz * blocks * rows, LANES)

    tok_float = tokens.astype(jnp.float32)
    stats = lax.psum(
        jnp.stack([jnp.sum(tok_float, axis=1), jnp.sum(tok_float * tok_float, axis=1)]), SEC
    )

    row_mean = stats[0] / model_width
    inv_std = lax.rsqrt(stats[1] / model_width - row_mean * row_mean + EPS)
    normed = (tok_float - row_mean[:, None]) * inv_std[:, None]
    hidden = (normed * gain[None, :]).astype(jnp.bfloat16)
    hidden_p, gout_p, gains_p = call(
        functools.partial(prepare_kernel, rows, nz),
        (
            pltpu.HBM((tok_rows, local_width), jnp.bfloat16),
            array((tok_rows, local_width)),
            array((16, local_width)),
        ),
        1_300_000_000,
        6_000_000,
        in_specs=[in_vmem, in_hbm, in_vmem],
        out_specs=(in_hbm, in_vmem, in_vmem),
        scratch_shapes=[
            pltpu.VMEM((tok_rows, local_width), jnp.bfloat16),
            pltpu.VMEM((tok_rows, local_width), jnp.bfloat16),
            pltpu.SemaphoreType.DMA((2,)),
        ],
    )(hidden, keep(grad_out), gain.reshape(1, local_width))
    own = lax.axis_index(FSDP) * rows
    own_gain = lax.dynamic_slice(gain, (own,), (rows,)).reshape(1, rows)

    along_z, hidden_p, gout_p, gains_p, own_gain = lax.optimization_barrier(
        (along_z, hidden_p, gout_p, gains_p, own_gain)
    )
    spread = call(
        functools.partial(spread_kernel, rows),
        array((nx * ny, nz * rows, width)),
        300_000_000,
        2_000_000,
    )(along_z)
    near = near_all_to_all(spread)

    near = near.reshape(nx, ny, nz * rows, width)
    half_rows = tok_rows // 2
    partial = call(
        project_kernel,
        array((2, half_rows + 8, width), jnp.float32),
        900_000_000,
        6_000_000,
        scratch_shapes=[pltpu.VMEM((local_width, width), jnp.bfloat16)],
    )(near, hidden_p, gout_p, gains_p)

    near, partial = lax.optimization_barrier((near, partial))
    half = lax.all_to_all(partial, "core", 0, 0)
    half = half[0] + half[1]
    near, half = lax.optimization_barrier((near, half))
    other = lax.ppermute(half, "xlo", [(0, 1), (1, 0)])
    weights = call(
        functools.partial(natural_kernel, rows, nz),
        array((local_width, cut)),
        460_000_000,
        3_000_000,
    )(near)
    half, weight_sums = call(
        add_kernel,
        (array((half_rows, width)), array((1, cut), jnp.float32)),
        300_000,
        1_400_000,
    )(half, other)
    both = lax.all_gather(half, "core", axis=0, tiled=True)

    both, weights = lax.optimization_barrier((both, weights))
    sent, grad_proj = call(
        attend_kernel,
        (array((nx, ny, nz * rows, width)), array((tok_rows, cut))),
        1_300_000_000,
        6_000_000,
        scratch_shapes=[pltpu.VMEM((tok_rows, head), jnp.bfloat16)],
    )(both, hidden_p, gout_p)

    received = near_all_to_all(sent.reshape(nx * ny, nz * rows, width))
    received, grad_proj, weight_sums = lax.optimization_barrier(
        (received, grad_proj, weight_sums)
    )
    folded = call(
        functools.partial(fold_kernel, rows),
        array((nz * blocks * rows, LANES)),
        300_000_000,
        2_000_000,
    )(received)
    folded = far_all_to_all(folded.reshape(nz, blocks * rows, LANES))
    grad_qkv, grad_outw_t, grad_gain = call(
        finish_kernel,
        (
            array((rows, cut), jnp.float32),
            array((rows, head), jnp.float32),
            array((1, rows), jnp.float32),
        ),
        10_000_000,
        300_000,
    )(folded, qkv_weight, own_gain)

    grad_hidden = lax.dot_general(
        grad_proj, weights, nt_dims, preferred_element_type=jnp.float32
    )
    proj_grad = grad_proj.astype(jnp.float32)
    first = jnp.sum(proj_grad * weight_sums, axis=1) / model_width
    second = jnp.sum(proj_grad * both[:, :cut].astype(jnp.float32), axis=1) / model_width
    grad_normed = grad_hidden * gain[None, :]
    grad_tokens = grad_out.astype(jnp.float32) + inv_std[:, None] * (
        grad_normed - first[:, None] - normed * second[:, None]
    )
    return (
        grad_tokens.astype(jnp.bfloat16),
        grad_qkv,
        grad_outw_t.T,
        grad_gain.reshape(rows),
    )


def solution(mesh):
    fine = Mesh(mesh.devices.reshape(2, 2, 4, 16, 2), SEC + FSDP)
    placed = (
        P(FSDP, SEC),
        P(FSDP, SEC),
        P(SEC),
        P(SEC + FSDP, None),
        P(None, SEC + FSDP),
    )
    return jax.shard_map(
        on_device,
        mesh=fine,
        in_specs=placed,
        out_specs=(
            P(FSDP, SEC),
            P(SEC + FSDP, None),
            P(None, SEC + FSDP),
            P(SEC + FSDP),
        ),
        check_vma=False,
    )
```

```python
import functools

import jax
import jax.numpy as jnp
from jax import lax
from jax.experimental import pallas as pl
from jax.experimental.pallas import tpu as pltpu
from jax.sharding import Mesh
from jax.sharding import PartitionSpec as P

PATCHES = 256


EPS = 1e-06

SEC = ("xlo", "core")
FSDP = ("y", "z", "xhi")
NEAR = ("core", "y", "xhi")
FAR = ("core", "z")
LANES = 128
VMEM_LIMIT = 28 * 1024 * 1024

nt_dims = (((1,), (1,)), ((), ()))
tn_dims = (((0,), (0,)), ((), ()))


def dot(a, b, dims=(((1,), (0,)), ((), ()))):
    return lax.dot_general(a, b, dims, preferred_element_type=jnp.float32)


def by_rows(index, rows):
    return lax.shift_right_logical(index * (65536 // rows + 1), jnp.full_like(index, 16))


def picks(shape, source_of_row):
    row = lax.broadcasted_iota(jnp.int32, shape, 0)
    column = lax.broadcasted_iota(jnp.int32, shape, 1)
    return (column == source_of_row(row)).astype(jnp.float32).astype(jnp.bfloat16)


def mirrored(index, count):
    return index + lax.axis_index("core") * (count - 1 - 2 * index)


def near_all_to_all(x):
    ny, nx = lax.axis_size("y"), lax.axis_size("xhi")
    groups = [
        [(c * ny + (y if c == 0 else ny - 1 - y)) * nx + h for h in range(nx) for y in range(ny)]
        for c in range(2)
    ]
    return lax.all_to_all(x, NEAR, 0, 0, axis_index_groups=groups)


def far_all_to_all(x):
    nz = lax.axis_size("z")
    groups = [list(range(nz)), list(range(2 * nz - 1, nz - 1, -1))]
    return lax.all_to_all(x, FAR, 0, 0, axis_index_groups=groups)


def unpack_block(rows, blocks, column_block, nz):
    def source(i):
        z = by_rows(i, rows)
        return mirrored(z, nz) * (rows * blocks) + column_block * rows + i - z * rows

    return source


def near_order(rows, nz):
    def source(i):
        z = by_rows(i, 2 * rows)
        rest = i - z * 2 * rows
        high = (rest >= rows).astype(jnp.int32)
        return high * (nz * rows) + z * rows + rest - high * rows

    return source


def pack_kernel(qkv_hbm, out_t_hbm, o_ref, qkv_ref, out_t_ref, sem):
    fetches = [
        pltpu.make_async_copy(qkv_hbm, qkv_ref, sem.at[0]),
        pltpu.make_async_copy(out_t_hbm, out_t_ref, sem.at[1]),
    ]
    for fetch in fetches:
        fetch.start()
    for fetch in fetches:
        fetch.wait()
    copies, span, _ = o_ref.shape
    rows = qkv_ref.shape[0]
    blocks = span // rows
    packed = jnp.zeros((span, LANES), jnp.float32)
    for b in range(blocks):
        pick = picks((span, rows), lambda i: i - b * rows)
        last = b == blocks - 1
        block = out_t_ref[...] if last else qkv_ref[:, b * LANES : (b + 1) * LANES]
        packed = packed + dot(pick, block)
    packed = packed.astype(jnp.bfloat16)
    for k in range(copies):
        o_ref[k] = packed


def spread_kernel(rows, x_ref, o_ref):
    copies, span, width = o_ref.shape
    blocks = width // LANES
    x = x_ref[...]
    for b in range(blocks):
        pick = picks((span, x.shape[0]), unpack_block(rows, blocks, b, span // rows))
        part = dot(pick, x).astype(jnp.bfloat16)
        for k in range(copies):
            o_ref[k, :, b * LANES : (b + 1) * LANES] = part


def prepare_kernel(rows, nz, hidden_ref, gain_ref, hp_ref, gains_ref):
    span = 2 * nz * rows
    pick = picks((span, span), near_order(rows, nz))
    for y in range(hidden_ref.shape[1] // span):
        at = slice(y * span, (y + 1) * span)
        hp_ref[:, at] = dot(hidden_ref[:, at], pick).astype(jnp.bfloat16)
        gain = gain_ref[:, at]
        high = gain.astype(jnp.bfloat16).astype(jnp.float32)
        row = lax.broadcasted_iota(jnp.int32, (16, span), 0)
        both = jnp.where(row == 0, high, jnp.where(row == 1, gain - high, 0.0))
        gains_ref[:, at] = dot(both.astype(jnp.bfloat16), pick).astype(jnp.bfloat16)


def project_kernel(
    rows, nz, near_ref, hidden_ref, gout_hbm, gain_ref, partial_ref, w_ref, gout_ref, sem
):
    fetch = pltpu.make_async_copy(gout_hbm, gout_ref, sem)
    fetch.start()
    nx, ny, part, width = near_ref.shape
    span = nx * part
    cut = width - LANES
    half = hidden_ref.shape[0] // 2
    pick = picks((span, span), near_order(rows, nz))
    for y in range(ny):
        listed = mirrored(y, ny)
        for x in range(nx):
            at = (y * nx + x) * part
            w_ref[at : at + part, :cut] = near_ref[x, listed, :, :cut]
        block = jnp.concatenate([near_ref[x, listed, :, cut:] for x in range(nx)], axis=0)
        w_ref[y * span : (y + 1) * span, cut:] = dot(pick, block).astype(jnp.bfloat16)
    sums = dot(gain_ref[...], w_ref[:, :cut])
    proj = dot(hidden_ref[...], w_ref[:, :cut])
    for h in range(2):
        partial_ref[h, half:, :cut] = sums[:8]
        partial_ref[h, half:, cut:] = jnp.zeros((8, LANES), jnp.float32)
        partial_ref[h, :half, :cut] = proj[h * half : (h + 1) * half]
    fetch.wait()
    att = dot(gout_ref[...], w_ref[:, cut:])
    for h in range(2):
        partial_ref[h, :half, cut:] = att[h * half : (h + 1) * half]


def natural_kernel(rows, nz, near_ref, gout_hbm, o_ref, gp_ref, gout_ref, sem):
    fetch = pltpu.make_async_copy(gout_hbm, gout_ref, sem)
    fetch.start()
    nx, ny, part, _ = near_ref.shape
    span = nx * part
    cut = o_ref.shape[1]
    pick = picks((span, span), near_order(rows, nz))
    for y in range(ny):
        block = jnp.concatenate([near_ref[x, mirrored(y, ny), :, :cut] for x in range(nx)], axis=0)
        o_ref[y * span : (y + 1) * span, :] = dot(pick, block).astype(jnp.bfloat16)
    fetch.wait()
    for y in range(ny):
        at = slice(y * span, (y + 1) * span)
        gp_ref[:, at] = dot(gout_ref[:, at], pick).astype(jnp.bfloat16)


def add_kernel(own_ref, other_ref, both_ref, sums_ref):
    count = both_ref.shape[0]
    both_ref[...] = (own_ref[:count] + other_ref[:count]).astype(jnp.bfloat16)
    cut = sums_ref.shape[1]
    tail = own_ref[count:, :cut] + other_ref[count:, :cut]
    sums_ref[...] = tail[0:1] + tail[1:2]


def attend_kernel(both_ref, hidden_ref, gout_ref, near_ref, gproj_ref, att_ref):
    nx, ny, part, width = near_ref.shape
    span = nx * part
    head = LANES
    scale = 1.0 / head**0.5
    for image in range(both_ref.shape[0] // PATCHES):
        at = slice(image * PATCHES, (image + 1) * PATCHES)
        query = both_ref[at, :head]
        key_in = both_ref[at, head : 2 * head]
        value = both_ref[at, 2 * head : 3 * head]
        grad_att = both_ref[at, 3 * head :]
        scores = dot(query, key_in, nt_dims) * scale
        raised = jnp.exp(scores - jnp.max(scores, axis=1, keepdims=True))
        probs = raised / jnp.sum(raised, axis=1, keepdims=True)
        probs_b = probs.astype(jnp.bfloat16)
        att_ref[at, :] = dot(probs_b, value).astype(jnp.bfloat16)
        grad_prob = dot(grad_att, value, nt_dims)
        inner = jnp.sum(grad_prob * probs, axis=1, keepdims=True)
        grad_score = (probs * (grad_prob - inner) * scale).astype(jnp.bfloat16)
        gproj_ref[at, :head] = dot(grad_score, key_in).astype(jnp.bfloat16)
        gproj_ref[at, head : 2 * head] = dot(grad_score, query, tn_dims).astype(jnp.bfloat16)
        gproj_ref[at, 2 * head :] = dot(probs_b, grad_att, tn_dims).astype(jnp.bfloat16)
    cut = width - head
    for y in range(ny):
        at = slice(y * span, (y + 1) * span)
        part_qkv = dot(hidden_ref[:, at], gproj_ref[...], tn_dims).astype(jnp.bfloat16)
        part_out = dot(gout_ref[:, at], att_ref[...], tn_dims).astype(jnp.bfloat16)
        for x in range(nx):
            listed = mirrored(y, ny)
            near_ref[x, listed, :, :cut] = part_qkv[x * part : (x + 1) * part]
            near_ref[x, listed, :, cut:] = part_out[x * part : (x + 1) * part]


def fold_kernel(rows, near_ref, o_ref):
    copies, span, width = near_ref.shape
    blocks = width // LANES
    total = near_ref[0].astype(jnp.float32)
    for k in range(1, copies):
        total = total + near_ref[k].astype(jnp.float32)
    total = total.astype(jnp.bfloat16)
    row = lax.broadcasted_iota(jnp.int32, (o_ref.shape[0], span), 0)
    column = lax.broadcasted_iota(jnp.int32, (o_ref.shape[0], span), 1)
    packed = jnp.zeros(o_ref.shape, jnp.float32)
    for b in range(blocks):
        pick = row == unpack_block(rows, blocks, b, span // rows)(column)
        pick = pick.astype(jnp.float32).astype(jnp.bfloat16)
        packed = packed + dot(pick, total[:, b * LANES : (b + 1) * LANES])
    o_ref[...] = packed.astype(jnp.bfloat16)


def finish_kernel(x_ref, qkv_ref, gain_ref, grad_ref, out_t_ref, gg_ref):
    rows = qkv_ref.shape[0]
    copies, span, _ = x_ref.shape
    x = x_ref[...].reshape(copies * span, LANES)
    blocks = span // rows
    row = lax.broadcasted_iota(jnp.int32, (rows, copies * span), 0)
    column = lax.broadcasted_iota(jnp.int32, (rows, copies * span), 1)
    within = column - by_rows(column, span) * span
    products = jnp.zeros((rows, LANES), jnp.float32)
    for b in range(blocks):
        pick = (within == row + b * rows).astype(jnp.float32).astype(jnp.bfloat16)
        part = dot(pick, x)
        if b == blocks - 1:
            out_t_ref[...] = part
        else:
            at = slice(b * LANES, (b + 1) * LANES)
            grad_ref[:, at] = part
            products = products + part * qkv_ref[:, at].astype(jnp.float32)
    ones = jnp.ones((8, LANES), jnp.float32)
    totals = lax.dot_general(
        ones,
        products,
        nt_dims,
        precision=lax.Precision.HIGHEST,
        preferred_element_type=jnp.float32,
    )
    gg_ref[...] = totals[:1] / gain_ref[...]


def call(kernel, out_shape, flops, moved, **more):
    return pl.pallas_call(
        kernel,
        out_shape=out_shape,
        compiler_params=pltpu.CompilerParams(vmem_limit_bytes=VMEM_LIMIT),
        cost_estimate=pl.CostEstimate(flops=flops, bytes_accessed=moved, transcendentals=0),
        **more,
    )


def array(shape, dtype=jnp.bfloat16):
    return jax.ShapeDtypeStruct(shape, dtype)


def on_device(tokens, grad_out, gain, qkv_weight, out_weight):
    tok_rows, local_width = tokens.shape
    model_width = local_width * lax.axis_size(SEC)
    head = out_weight.shape[0]
    rows = qkv_weight.shape[0]
    ny, nz, nx = (lax.axis_size(a) for a in FSDP)
    cut = 3 * head
    width = cut + head
    blocks = width // LANES

    in_hbm = pl.BlockSpec(memory_space=pltpu.HBM)
    in_vmem = pl.BlockSpec(memory_space=pltpu.VMEM)

    def keep(x):
        return pltpu.with_memory_space_constraint(x, pltpu.HBM)

    packed = call(
        pack_kernel,
        array((nz, blocks * rows, LANES)),
        1_000_000,
        200_000,
        in_specs=[in_hbm, in_hbm],
        scratch_shapes=[
            pltpu.VMEM((rows, cut), jnp.bfloat16),
            pltpu.VMEM((rows, head), jnp.bfloat16),
            pltpu.SemaphoreType.DMA((2,)),
        ],
    )(keep(qkv_weight), keep(out_weight.T))
    along_z = far_all_to_all(packed).reshape(nz * blocks * rows, LANES)

    tok_float = tokens.astype(jnp.float32)
    stats = lax.psum(
        jnp.stack([jnp.sum(tok_float, axis=1), jnp.sum(tok_float * tok_float, axis=1)]), SEC
    )

    row_mean = stats[0] / model_width
    inv_std = lax.rsqrt(stats[1] / model_width - row_mean * row_mean + EPS)
    normed = (tok_float - row_mean[:, None]) * inv_std[:, None]
    hidden = (normed * gain[None, :]).astype(jnp.bfloat16)
    hidden_p, gains_p = call(
        functools.partial(prepare_kernel, rows, nz),
        (array((tok_rows, local_width)), array((16, local_width))),
        700_000_000,
        3_000_000,
    )(hidden, gain.reshape(1, local_width))
    fetched = [pltpu.VMEM((tok_rows, local_width), jnp.bfloat16), pltpu.SemaphoreType.DMA]
    own = lax.axis_index(FSDP) * rows
    own_gain = lax.dynamic_slice(gain, (own,), (rows,)).reshape(1, rows)

    along_z, hidden_p, gains_p, own_gain = lax.optimization_barrier(
        (along_z, hidden_p, gains_p, own_gain)
    )
    spread = call(
        functools.partial(spread_kernel, rows),
        array((nx * ny, nz * rows, width)),
        300_000_000,
        2_000_000,
    )(along_z)
    near = near_all_to_all(spread)

    near = near.reshape(nx, ny, nz * rows, width)
    half_rows = tok_rows // 2
    partial = call(
        functools.partial(project_kernel, rows, nz),
        array((2, half_rows + 8, width), jnp.float32),
        900_000_000,
        6_000_000,
        in_specs=[in_vmem, in_vmem, in_hbm, in_vmem],
        scratch_shapes=[pltpu.VMEM((local_width, width), jnp.bfloat16)] + fetched,
    )(near, hidden_p, keep(grad_out), gains_p)

    near, partial = lax.optimization_barrier((near, partial))
    half = lax.all_to_all(partial, "core", 0, 0)
    half = half[0] + half[1]
    near, half = lax.optimization_barrier((near, half))
    other = lax.ppermute(half, "xlo", [(0, 1), (1, 0)])
    weights, gout_p = call(
        functools.partial(natural_kernel, rows, nz),
        (array((local_width, cut)), array((tok_rows, local_width))),
        1_060_000_000,
        6_000_000,
        in_specs=[in_vmem, in_hbm],
        scratch_shapes=fetched,
    )(near, keep(grad_out))
    half, weight_sums = call(
        add_kernel,
        (array((half_rows, width)), array((1, cut), jnp.float32)),
        300_000,
        1_400_000,
    )(half, other)
    both = lax.all_gather(half, "core", axis=0, tiled=True)

    both, weights, gout_p = lax.optimization_barrier((both, weights, gout_p))
    sent, grad_proj = call(
        attend_kernel,
        (array((nx, ny, nz * rows, width)), array((tok_rows, cut))),
        1_300_000_000,
        6_000_000,
        scratch_shapes=[pltpu.VMEM((tok_rows, head), jnp.bfloat16)],
    )(both, hidden_p, gout_p)

    received = near_all_to_all(sent.reshape(nx * ny, nz * rows, width))
    received, grad_proj, weight_sums = lax.optimization_barrier(
        (received, grad_proj, weight_sums)
    )
    folded = call(
        functools.partial(fold_kernel, rows),
        array((nz * blocks * rows, LANES)),
        300_000_000,
        2_000_000,
    )(received)
    folded = far_all_to_all(folded.reshape(nz, blocks * rows, LANES))
    grad_qkv, grad_outw_t, grad_gain = call(
        finish_kernel,
        (
            array((rows, cut), jnp.float32),
            array((rows, head), jnp.float32),
            array((1, rows), jnp.float32),
        ),
        10_000_000,
        300_000,
    )(folded, qkv_weight, own_gain)

    grad_hidden = lax.dot_general(
        grad_proj, weights, nt_dims, preferred_element_type=jnp.float32
    )
    proj_grad = grad_proj.astype(jnp.float32)
    first = jnp.sum(proj_grad * weight_sums, axis=1) / model_width
    second = jnp.sum(proj_grad * both[:, :cut].astype(jnp.float32), axis=1) / model_width
    grad_normed = grad_hidden * gain[None, :]
    grad_tokens = grad_out.astype(jnp.float32) + inv_std[:, None] * (
        grad_normed - first[:, None] - normed * second[:, None]
    )
    return (
        grad_tokens.astype(jnp.bfloat16),
        grad_qkv,
        grad_outw_t.T,
        grad_gain.reshape(rows),
    )


def solution(mesh):
    fine = Mesh(mesh.devices.reshape(2, 2, 4, 16, 2), SEC + FSDP)
    placed = (
        P(FSDP, SEC),
        P(FSDP, SEC),
        P(SEC),
        P(SEC + FSDP, None),
        P(None, SEC + FSDP),
    )
    return jax.shard_map(
        on_device,
        mesh=fine,
        in_specs=placed,
        out_specs=(
            P(FSDP, SEC),
            P(SEC + FSDP, None),
            P(None, SEC + FSDP),
            P(SEC + FSDP),
        ),
        check_vma=False,
    )
```
